32 devices in a mesh: slab: 4 (over x, core), chan: 8 (over z, y).
Axes of the slice: x: 2, y: 2, z: 4, core: 2. Of those that a mesh axis runs over, the one named last changes fastest.
Arguments:
- inputs: bfloat16 [512, 32, 256], P('chan', 'slab'), may hold values from -6 to 6
- weights: bfloat16 [27, 512, 512], P(None, 'chan', 'slab'), may hold values from -0.0546875 to 0.0546875
- cotangent: bfloat16 [512, 32, 256], P('chan', 'slab'), may hold values from -6 to 6
Outputs:
- outputs: bfloat16 [512, 32, 256], P('chan', 'slab')
- gradient: bfloat16 [512, 32, 256], P('chan', 'slab')
The draws below stay inside these ranges and needn't reach their ends.
All inputs are finite; a program needn't handle non-finite values.
Results may differ from the reference program's by a relative error of at most 0.0014.
Values may be sent and summed in bfloat16 or wider, within the bound.
A program may use at most 64 MiB of HBM per device.

```python
import jax
import jax.numpy as jnp
from jax import lax

C = 512
ROWS = 8
COLS = 32
DEPTH = 32


def block_scale(stream_key, dims, cuts, smallest, high):
    gain = 1.0
    for dim, blocks in cuts:
        steps = jax.random.uniform(jax.random.fold_in(jax.random.fold_in(stream_key, 6), dim), (blocks,), jnp.float32, smallest / len(cuts), high / len(cuts))
        gain = gain * jnp.repeat(jnp.exp(steps), dims[dim] // blocks).reshape((-1,) + (1,) * (len(dims) - 1 - dim))
    return gain


def bell_draw(stream_key, extent, scale, bound, shards=(), dtype=jnp.bfloat16):
    values = scale * jax.random.normal(stream_key, extent, jnp.float32)
    if shards:
        values = values * block_scale(stream_key, extent, shards, -0.22, 0.18)
    return jnp.clip(values, -bound, bound).astype(dtype)


def setup_inputs(seed: int = 0) -> dict:
    keys = jax.random.split(jax.random.key(seed), 4)
    inputs = bell_draw(keys[0], (C, DEPTH, ROWS * COLS), 1.0, 6.0, ((0, 8), (1, 4)))
    weights = bell_draw(keys[1], (27, C, C), (27 * C) ** -0.5, 0.0546875, ((1, 8), (2, 4)))
    cotangent = bell_draw(keys[2], (C, DEPTH, ROWS * COLS), 1.0, 6.0, ((0, 8), (1, 4)))
    return {"inputs": inputs, "weights": weights, "cotangent": cotangent}


def convolve(volume, kernel):
    channels = volume.shape[0]
    shaped = volume.reshape(1, channels, volume.shape[1], ROWS, COLS)
    filters = jnp.transpose(kernel, (1, 2, 0)).reshape(kernel.shape[1], kernel.shape[2], 3, 3, 3)
    result = lax.conv_general_dilated(shaped, filters, (1, 1, 1), ((1, 1), (1, 1), (1, 1)), dimension_numbers=('NCDHW', 'OIDHW', 'NCDHW'), precision=lax.Precision.HIGHEST)
    return result.reshape(kernel.shape[1], volume.shape[1], ROWS * COLS)

def reference(inputs, weights, cotangent):
    volume_in = inputs.astype(jnp.float32)
    kernel_in = weights.astype(jnp.float32)

    def forward(field_in):
        return convolve(field_in, kernel_in)
    result, pullback = jax.vjp(forward, volume_in)
    grad_in = pullback(cotangent.astype(jnp.float32))[0]
    return (result.astype(jnp.bfloat16), grad_in.astype(jnp.bfloat16))
```

```python
import functools

import jax
import jax.numpy as jnp
from jax import lax
from jax.experimental import pallas as pl
from jax.experimental.pallas import tpu as pltpu
from jax.sharding import PartitionSpec as P

ROWS = 8
COLS = 32
TAPS = 27
LANES = 128
H = 2


def when(cond, fn):
    if cond is None:
        fn()
    else:
        pl.when(cond)(fn)


def both(a, b):
    return b if a is None else a if b is None else jnp.logical_and(a, b)


def gather_kernel(S, Z, Y, r, x_ref, w_ref, p_ref, g_ref, wf_ref, wg_ref,
                  lsem, vsend, ysend, vrecv, hsend, hrecv, wsend, wrecv, psend, fsend, xsend, precv):
    n = Z * Y
    planes = x_ref.shape[1]
    units, part = 2 * H, planes // H
    s, c = lax.axis_index("slab"), lax.axis_index("chan")
    z, y = lax.div(c, Y), lax.rem(c, Y)
    core = lax.rem(s, 2)
    mate = s + 1 - 2 * core
    ypeer = [z * Y + lax.rem(y + j, Y) for j in range(1, Y)]
    up, down = z < Z - 1, z > 0

    barrier = pltpu.get_barrier_semaphore()
    links = [(up, (s, c + Y)), (down, (s, c - Y))]
    links += [(None, (s, peer)) for peer in ypeer]
    links += [(None, (lax.rem(s + j, S), c)) for j in range(1, S)]
    targets = []
    pair = S // 2
    x = lax.div(s, 2)
    host = 2 * lax.rem(lax.div(c, 2), pair) + lax.rem(c, 2)
    for j in range(r):
        to = (host, s * r + j)
        targets.append((jnp.logical_or(to[0] != s, to[1] != c), to, j, j))
    sources = []
    for k in range(n // 2):
        frm = (lax.div(c, r), 2 * k + core)
        other = jnp.logical_or(frm[0] != s, frm[1] != c)
        sources.append((jnp.logical_and(other, x == k % pair), frm))
    links += [(t[0], t[1]) for t in targets] + sources
    for cond, peer in links:
        when(cond, functools.partial(pl.semaphore_signal, barrier, inc=1, device_id=peer,
                                     device_id_type=pl.DeviceIdType.MESH))
    peers = sum(1 if cond is None else cond.astype(jnp.int32) for cond, _ in links)
    pl.semaphore_wait(barrier, peers)

    sent = []

    def send(cond, src, dst, ssem, rsem, to):
        def make():
            return pltpu.make_async_remote_copy(src_ref=src, dst_ref=dst, send_sem=ssem, recv_sem=rsem,
                                                device_id=to, device_id_type=pl.DeviceIdType.MESH)
        when(cond, lambda: make().start())
        sent.append((cond, make))

    def arrive(cond, dst, sem):
        when(cond, lambda: pltpu.make_async_copy(dst, dst, sem).wait())

    def own(u):
        return x_ref.at[u // H, pl.ds(u % H * part, part)]

    def block(u, slot):
        return g_ref.at[u // H, pl.ds(1 + u % H * part, part), slot]

    def along(cond, u, slot, src, side):
        ok, to = (up, (s, c + Y)) if side == 0 else (down, (s, c - Y))
        send(both(cond, ok), src, block(u, slot), vsend.at[u, side, slot], vrecv.at[u, slot], to)

    def across(cond, u, slot, src):
        for j, peer in enumerate(ypeer):
            send(cond, src, block(u, slot), ysend.at[u, j, slot], vrecv.at[u, slot], (s, peer))

    def landed(cond, u, slot):
        arrive(cond, block(u, slot), vrecv.at[u, slot])

    def rim(cond, u, slot, first=None, last=None):
        v = u // H
        if u % H == H - 1:
            last = g_ref.at[v, planes, slot] if last is None else last
            send(both(cond, s < S - 1), last, g_ref.at[v, 0, slot], hsend.at[v, 0, slot], hrecv.at[v, 0, slot],
                 (s + 1, c))
        if u % H == 0:
            first = g_ref.at[v, 1, slot] if first is None else first
            send(both(cond, s > 0), first, g_ref.at[v, planes + 1, slot], hsend.at[v, 1, slot], hrecv.at[v, 1, slot],
                 (s - 1, c))

    for u in range(units):
        for side in range(2):
            along(None, u, c, own(u), side)
        across(None, u, c, own(u))
        if u == H - 1:
            for cond, to, j, k in targets:
                send(cond, p_ref.at[j], wg_ref.at[c], psend.at[k], precv.at[c], to)
    for j in range(1, S // 2):
        send(None, w_ref, wf_ref.at[s], wsend.at[j], wrecv.at[s], (lax.rem(s + 2 * j, S), c))
    send(None, w_ref, wf_ref.at[s], wsend.at[0], wrecv.at[s], (mate, c))
    for u in range(units):
        pltpu.make_async_copy(own(u), block(u, c), lsem.at[u]).start()
        rim(None, u, c, x_ref.at[u // H, 0], x_ref.at[u // H, planes - 1])
    pltpu.make_async_copy(w_ref, wf_ref.at[s], lsem.at[units]).start()
    home = jnp.logical_and(s == lax.div(c, r), s == host)
    when(home, lambda: pltpu.make_async_copy(p_ref.at[lax.rem(c, r)], wg_ref.at[c], precv.at[c]).start())

    for side in range(2):
        def clear(side=side):
            for v in range(2):
                row = 0 if side == 0 else planes + 1
                g_ref[v, row] = jnp.zeros(g_ref.shape[2:], g_ref.dtype)
        when(s == (0 if side == 0 else S - 1), clear)

    for k in range(1, Z):
        for u in range(units):
            for side in range(2):
                zz = z - k if side == 0 else z + k
                have = zz >= 0 if side == 0 else zz < Z
                slot = zz * Y + y
                landed(have, u, slot)
                if k < Z - 1:
                    along(have, u, slot, block(u, slot), side)
                across(have, u, slot, block(u, slot))
                rim(have, u, slot)
        if k == 1:
            for j in range(1, S // 2):
                slot = lax.rem(s + 2 * j, S)
                arrive(None, wf_ref.at[slot], wrecv.at[slot])
                send(None, wf_ref.at[slot], wf_ref.at[slot], wsend.at[S // 2 + j], wrecv.at[slot], (mate, c))
    for direct in range(2):
        for k in range(n // 2):
            slot = 2 * k + core
            have = x == k % pair if direct == 0 else x != k % pair
            piece = wg_ref.at[slot]
            arrive(have, piece, precv.at[slot])
            if direct == 0:
                for j in range(1, pair):
                    send(have, piece, piece, xsend.at[j, k], precv.at[slot], (lax.rem(s + 2 * j, S), c))
            send(have, piece, piece, fsend.at[k], precv.at[slot], (mate, c))
    for k in range(Z):
        for u in range(units):
            for peer in ypeer:
                for side in range(2 if k else 1):
                    zz = z - k if side == 0 else z + k
                    have = None if k == 0 else zz >= 0 if side == 0 else zz < Z
                    slot = zz * Y + peer - z * Y
                    landed(have, u, slot)
                    rim(have, u, slot)
    for u in range(units):
        pltpu.make_async_copy(own(u), block(u, c), lsem.at[u]).wait()
    pltpu.make_async_copy(w_ref, wf_ref.at[s], lsem.at[units]).wait()
    for j in range(S // 2):
        slot = lax.rem(mate + 2 * j, S)
        arrive(None, wf_ref.at[slot], wrecv.at[slot])
    for k in range(n // 2):
        slot = 2 * k + 1 - core
        arrive(None, wg_ref.at[slot], precv.at[slot])
    for v in range(2):
        for slot in range(n):
            arrive(s > 0, g_ref.at[v, 0, slot], hrecv.at[v, 0, slot])
            arrive(s < S - 1, g_ref.at[v, planes + 1, slot], hrecv.at[v, 1, slot])
    for cond, make in sent:
        when(cond, lambda make=make: make().wait_send())


def conv_kernel(g_ref, wf_ref, wg_ref, o_ref, k_ref):
    S, _, lc, width = wf_ref.shape
    n = wg_ref.shape[0]
    planes = o_ref.shape[1]
    cells = o_ref.shape[3]
    pack = LANES // lc
    for t in range(TAPS):
        rows = pl.ds(t * lc, lc)
        k_ref[0, rows, :] = jnp.concatenate([wf_ref[i, t] for i in range(S)], axis=-1)
        f = TAPS - 1 - t
        at = (f % pack) * lc
        k_ref[1, rows, :] = jnp.concatenate([wg_ref[i, f // pack][:, at:at + lc] for i in range(n)], axis=-1)
    lane = lax.broadcasted_iota(jnp.int32, (lc, cells), 1)
    row, col = lane // COLS, lane % COLS
    nine = 9 * lc

    def step(k, carry):
        v, d = k // planes, k % planes
        total = None
        for a in range(3):
            part = jnp.dot(k_ref[v, pl.ds(a * nine, nine), :], g_ref[v, d + a], preferred_element_type=jnp.float32)
            total = part if total is None else total + part
        result = None
        for b in range(3):
            lines = None
            for c in range(3):
                at = (3 * b + c) * lc
                piece = total[at:at + lc]
                if c != 1:
                    piece = pltpu.roll(piece, (1 - c) % cells, 1)
                    piece = jnp.where(col == (0 if c == 0 else COLS - 1), 0.0, piece)
                lines = piece if lines is None else lines + piece
            if b != 1:
                lines = pltpu.roll(lines, ((1 - b) * COLS) % cells, 1)
                lines = jnp.where(row == (0 if b == 0 else ROWS - 1), 0.0, lines)
            result = lines if result is None else result + lines
        o_ref[v, d] = result.astype(o_ref.dtype)
        return carry

    lax.fori_loop(0, 2 * planes, step, 0)


def general(S, n, inputs, weights, cotangent):
    lc, planes, cells = inputs.shape
    wide = weights.shape[2]
    r = wide // lc
    C = n * lc
    Y = max(d for d in range(1, n + 1) if n % d == 0 and 2 * d * d <= n)
    Z = n // Y
    volumes = jnp.stack((inputs, cotangent)).transpose(0, 2, 1, 3)
    pack = LANES // lc
    nt = -(-TAPS // pack)
    padded = jnp.pad(weights, ((0, nt * pack - TAPS), (0, 0), (0, 0)))
    pieces = padded.reshape(nt, pack, lc, r, lc).transpose(3, 0, 4, 1, 2).reshape(r, nt, lc, pack * lc)
    vmem = pl.BlockSpec(memory_space=pltpu.VMEM)
    anyspace = pl.BlockSpec(memory_space=pl.ANY)
    dma = pltpu.SemaphoreType.DMA
    bf16 = jnp.bfloat16
    gathered, wf, wg = pl.pallas_call(
        functools.partial(gather_kernel, S, Z, Y, r),
        out_shape=(jax.ShapeDtypeStruct((2, planes + 2, n, lc, cells), bf16),
                   jax.ShapeDtypeStruct((S,) + weights.shape, bf16),
                   jax.ShapeDtypeStruct((n,) + pieces.shape[1:], bf16)),
        in_specs=[anyspace] * 3,
        out_specs=(vmem,) * 3,
        scratch_shapes=[dma((2 * H + 1,)), dma((2 * H, 2, n)), dma((2 * H, Y - 1, n)), dma((2 * H, n)), dma((2, 2, n)), dma((2, 2, n)),
                        dma((S,)), dma((S,)), dma((r,)), dma((n // 2,)), dma((S // 2, n // 2)), dma((n,))],
        compiler_params=pltpu.CompilerParams(collective_id=0, has_side_effects=True, vmem_limit_bytes=40 << 20),
        name="gather",
    )(volumes, weights, pieces)
    out = pl.pallas_call(
        conv_kernel,
        out_shape=jax.ShapeDtypeStruct((2, planes, lc, cells), bf16),
        in_specs=[vmem] * 3,
        out_specs=vmem,
        scratch_shapes=[pltpu.VMEM((2, TAPS * lc, C), bf16)],
        compiler_params=pltpu.CompilerParams(vmem_limit_bytes=48 << 20),
        name="conv",
    )(gathered.reshape(2, planes + 2, C, cells), wf, wg)
    out = out.transpose(0, 2, 1, 3)
    return out[0], out[1]


def ranges(planes):
    return [(planes - 1, 1)] + [(p, 2) for p in range(0, planes - 2, 2)] + [(planes - 2, 1)]


def split_kernel(x_ref, w_ref, out_ref, g_ref, wst_ref, k_ref, ob_ref,
                 asend, arecv, ysend, hsend, hrecv, wsend, wrecv, osend, orecv):
    planes, n = ob_ref.shape[0], g_ref.shape[1]
    lc, cells = g_ref.shape[2:]
    C = n * lc
    wide = w_ref.shape[2]
    chunks = ranges(planes)
    s, c = lax.axis_index("slab"), lax.axis_index("chan")
    z, y = lax.div(c, 2), lax.rem(c, 2)
    x, core = lax.div(s, 2), lax.rem(s, 2)
    h = lax.div(z, 2)
    outer = lax.rem(z, 3) == 0
    inner = jnp.logical_not(outer)
    odd = lax.rem(z + y, 2) == 1
    even = jnp.logical_not(odd)
    b = z - 2 * h
    zp = 4 * h + 1 - z
    v = jnp.where(outer, 0, 1)
    mate, xpeer = s + 1 - 2 * core, s + 2 - 4 * x
    ypeer = 2 * z + 1 - y
    MESH = pl.DeviceIdType.MESH

    side = jnp.where(outer, x, 1 - x)
    goal = (2 * side + h, 2 * (1 + x) + core)
    zin = jnp.where(x == h, 3 * core, 1 + core)
    ring = [lax.rem(z + j, 4) for j in range(1, 4)]

    links = [(None, (mate, c)), (None, (xpeer, c)), (None, (s, ypeer))]
    links += [(None, (s, 2 * zz + y)) for zz in ring]
    links += [(x != core, (3 - s, c)), (odd, (s, 2 * zp + 1 - y)), (None, goal)]
    links += [(inner, (2 * h + y, 2 * zin + yy)) for yy in range(2)]
    barrier = pltpu.get_barrier_semaphore()
    for cond, peer in links:
        when(cond, functools.partial(pl.semaphore_signal, barrier, inc=1, device_id=peer, device_id_type=MESH))
    pl.semaphore_wait(barrier, sum(1 if cond is None else cond.astype(jnp.int32) for cond, _ in links))

    sent = []

    def send(cond, src, dst, ssem, rsem, to):
        def make():
            return pltpu.make_async_remote_copy(src_ref=src, dst_ref=dst, send_sem=ssem, recv_sem=rsem,
                                                device_id=to, device_id_type=MESH)
        when(cond, lambda: make().start())
        sent.append((cond, make))

    def local(cond, src, dst, sem):
        when(cond, lambda: pltpu.make_async_copy(src, dst, sem).start())

    def arrive(cond, dst, sem):
        when(cond, lambda: pltpu.make_async_copy(dst, dst, sem).wait())

    def shard(p, q):
        return wst_ref.at[p, :, pl.ds(q * lc, lc) if isinstance(q, int) else pl.ds(pl.multiple_of(q * lc, lc), lc)]

    def block(i, slot):
        return g_ref.at[pl.ds(1 + chunks[i][0], chunks[i][1]), slot]

    def own(u, i):
        return x_ref.at[u, pl.ds(*chunks[i])]

    send(None, w_ref, shard(z, y), wsend.at[0], wrecv.at[z, y], goal)
    send(inner, w_ref, shard(s, b), wsend.at[1], wrecv.at[s, b], (s, 2 * zp + y))
    local(outer, w_ref, shard(s, b), wrecv.at[s, b])
    for i in range(len(chunks)):
        for zz in ring:
            send(None, own(jnp.where(lax.rem(zz, 3) == 0, 0, 1), i), block(i, c), asend.at[i, zz], arecv.at[i, c],
                 (s, 2 * zz + y))
        send(None, own(v, i), block(i, c), ysend.at[i, z], arecv.at[i, c], (s, ypeer))
        local(None, own(v, i), block(i, c), arecv.at[i, c])
    for edge in range(2):
        def clear(edge=edge):
            row = 0 if edge == 0 else planes + 1
            g_ref[row] = jnp.zeros(g_ref.shape[1:], g_ref.dtype)
        when(s == (0 if edge == 0 else 3), clear)

    def rim(i, slot):
        first, count = chunks[i]
        if first + count == planes:
            send(s < 3, g_ref.at[planes, slot], g_ref.at[0, slot], hsend.at[0, slot], hrecv.at[0, slot], (s + 1, c))
        if first == 0:
            send(s > 0, g_ref.at[1, slot], g_ref.at[planes + 1, slot], hsend.at[1, slot], hrecv.at[1, slot],
                 (s - 1, c))

    def column(i):
        for j, zz in enumerate([z, *ring]):
            slot = 2 * zz + y
            arrive(None, block(i, slot), arecv.at[i, slot])
            if j:
                send(None, block(i, slot), block(i, slot), ysend.at[i, zz], arecv.at[i, slot], (s, ypeer))
            rim(i, slot)

    def across(i):
        for zz in [z, *ring]:
            slot = 2 * zz + 1 - y
            arrive(None, block(i, slot), arecv.at[i, slot])
            rim(i, slot)

    def pair(k):
        so = [s, mate, xpeer, 3 - s][k]
        zi = [zin, jnp.where(x == h, 3 * (1 - core), 2 - core), jnp.where(x == h, 1 + core, 3 * core),
              jnp.where(x == h, 2 - core, 3 * (1 - core))][k]
        return jnp.where(outer, so, zi)

    def weights(k):
        p = pair(k)
        for q in range(2):
            arrive(None, shard(p, q), wrecv.at[p, q])
            if k == 0:
                send(None, shard(p, q), shard(p, q), wsend.at[2 + q], wrecv.at[p, q], (xpeer, c))
            if k % 2 == 0:
                send(None, shard(p, q), shard(p, q), wsend.at[4 + k + q], wrecv.at[p, q], (mate, c))

    def build(k):
        p = pair(k)
        at = pl.multiple_of(p * 2 * lc, 2 * lc)
        for a in range(3):
            def tap(t, carry, a=a):
                rows = pl.ds(pl.multiple_of(t * 2 * lc, 2 * lc), 2 * lc)
                cols = pl.ds(pl.multiple_of(a * C + at, 2 * lc), 2 * lc)

                def plain():
                    k_ref[rows, cols] = wst_ref[p, 9 * a + t]

                def turned():
                    k_ref[rows, cols] = wst_ref[p, TAPS - 1 - 9 * a - t].T
                pl.when(outer)(plain)
                pl.when(inner)(turned)
                return carry
            lax.fori_loop(0, 9, tap, 0)

    lane = lax.broadcasted_iota(jnp.int32, (2 * lc, cells), 1)
    row, col = lane // COLS, lane % COLS

    def convolve(d, carry):
        rhs = g_ref[pl.ds(d, 3)].reshape(3 * C, cells)
        total = jnp.dot(k_ref[...], rhs, preferred_element_type=jnp.float32)
        result = None
        for t in range(3):
            lines = None
            for u in range(3):
                at = (3 * t + u) * 2 * lc
                piece = total[at:at + 2 * lc]
                if u != 1:
                    piece = pltpu.roll(piece, (1 - u) % cells, 1)
                    piece = jnp.where(col == (0 if u == 0 else COLS - 1), 0.0, piece)
                lines = piece if lines is None else lines + piece
            if t != 1:
                lines = pltpu.roll(lines, ((1 - t) * COLS) % cells, 1)
                lines = jnp.where(row == (0 if t == 0 else ROWS - 1), 0.0, lines)
            result = lines if result is None else result + lines
        ob_ref[d] = result.reshape(2, lc, cells).astype(ob_ref.dtype)
        return carry

    home = z == 2 * h + y

    def deliver(d):
        for q in range(2):
            dst = out_ref.at[v, d]
            stay = jnp.where(outer, b == q, jnp.logical_and(home, y == q))
            to = (s, jnp.where(outer, 2 * (2 * h + q) + y, 2 * (2 * h + y) + q))
            send(jnp.logical_not(stay), ob_ref.at[d, q], dst, osend.at[d, q], orecv.at[v, d], to)
            local(stay, ob_ref.at[d, q], dst, orecv.at[v, d])

    def run(lo, hi):
        def one(d, carry):
            convolve(d, carry)
            return carry
        lax.fori_loop(lo, hi, one, 0)
        for d in range(lo, hi):
            deliver(d)

    last = len(chunks) - 1
    weights(0)
    column(0)
    column(1)
    build(0)
    weights(1)
    build(1)
    across(0)
    across(1)
    column(2)
    weights(2)
    across(2)
    build(2)
    column(3)
    weights(3)
    build(3)
    for edge in range(2):
        for slot in range(n):
            arrive((s > 0) if edge == 0 else (s < 3), g_ref.at[0 if edge == 0 else planes + 1, slot],
                   hrecv.at[edge, slot])
    run(0, 3)
    for i in range(4, len(chunks)):
        column(i)
    across(3)
    run(3, 5)
    for i in range(4, len(chunks)):
        across(i)
    run(5, planes)
    for d in range(planes):
        for u in range(2):
            arrive(None, out_ref.at[u, d], orecv.at[u, d])
    for cond, make in sent:
        when(cond, lambda make=make: make().wait_send())


def split(n, inputs, weights, cotangent):
    lc, planes, cells = inputs.shape
    volumes = jnp.stack((inputs, cotangent)).transpose(0, 2, 1, 3)
    dma = pltpu.SemaphoreType.DMA
    bf16 = jnp.bfloat16
    count = len(ranges(planes))
    out = pl.pallas_call(
        split_kernel,
        out_shape=jax.ShapeDtypeStruct((2, planes, lc, cells), bf16),
        in_specs=[pl.BlockSpec(memory_space=pl.ANY)] * 2,
        out_specs=pl.BlockSpec(memory_space=pltpu.VMEM),
        scratch_shapes=[pltpu.VMEM((planes + 2, n, lc, cells), bf16),
                        pltpu.VMEM((n // 2, TAPS, 2 * lc, weights.shape[2]), bf16),
                        pltpu.VMEM((9 * 2 * lc, 3 * n * lc), bf16),
                        pltpu.VMEM((planes, 2, lc, cells), bf16),
                        dma((count, 4)), dma((count, n)), dma((count, 4)), dma((2, n)), dma((2, n)),
                        dma((8,)), dma((n // 2, 2)), dma((planes, 2)), dma((2, planes))],
        compiler_params=pltpu.CompilerParams(collective_id=1, has_side_effects=True, vmem_limit_bytes=48 << 20),
        name="split",
    )(volumes, weights)
    out = out.transpose(0, 2, 1, 3)
    return out[0], out[1]


def body(S, n, inputs, weights, cotangent):
    lc = inputs.shape[0]
    if (S, n) == (4, 8) and weights.shape[2] == 2 * lc == LANES and inputs.shape[1] == 8:
        return split(n, inputs, weights, cotangent)
    return general(S, n, inputs, weights, cotangent)


def solution(mesh):
    S, n = mesh.shape["slab"], mesh.shape["chan"]
    return jax.shard_map(
        functools.partial(body, S, n),
        mesh=mesh,
        in_specs=(P("chan", "slab", None), P(None, "chan", "slab"), P("chan", "slab", None)),
        out_specs=(P("chan", "slab", None), P("chan", "slab", None)),
        check_vma=False,
    )
```

```python
import functools

import jax
import jax.numpy as jnp
from jax import lax
from jax.experimental import pallas as pl
from jax.experimental.pallas import tpu as pltpu
from jax.sharding import PartitionSpec as P

ROWS = 8
COLS = 32
TAPS = 27
LANES = 128
H = 2
PIECES = 3


def when(cond, fn):
    if cond is None:
        fn()
    else:
        pl.when(cond)(fn)


def both(a, b):
    return b if a is None else a if b is None else jnp.logical_and(a, b)


def gather_kernel(S, Z, Y, r, x_ref, w_ref, p_ref, g_ref, wf_ref, wg_ref,
                  lsem, vsend, ysend, vrecv, hsend, hrecv, wsend, wrecv, psend, fsend, xsend, precv):
    n = Z * Y
    planes = x_ref.shape[1]
    units, part = 2 * H, planes // H
    s, c = lax.axis_index("slab"), lax.axis_index("chan")
    z, y = lax.div(c, Y), lax.rem(c, Y)
    core = lax.rem(s, 2)
    mate = s + 1 - 2 * core
    ypeer = [z * Y + lax.rem(y + j, Y) for j in range(1, Y)]
    up, down = z < Z - 1, z > 0

    barrier = pltpu.get_barrier_semaphore()
    links = [(up, (s, c + Y)), (down, (s, c - Y))]
    links += [(None, (s, peer)) for peer in ypeer]
    links += [(None, (lax.rem(s + j, S), c)) for j in range(1, S)]
    targets = []
    pair = S // 2
    x = lax.div(s, 2)
    host = 2 * lax.rem(lax.div(c, 2), pair) + lax.rem(c, 2)
    for j in range(r):
        to = (host, s * r + j)
        targets.append((jnp.logical_or(to[0] != s, to[1] != c), to, j, j))
    sources = []
    for k in range(n // 2):
        frm = (lax.div(c, r), 2 * k + core)
        other = jnp.logical_or(frm[0] != s, frm[1] != c)
        sources.append((jnp.logical_and(other, x == k % pair), frm))
    links += [(t[0], t[1]) for t in targets] + sources
    for cond, peer in links:
        when(cond, functools.partial(pl.semaphore_signal, barrier, inc=1, device_id=peer,
                                     device_id_type=pl.DeviceIdType.MESH))
    peers = sum(1 if cond is None else cond.astype(jnp.int32) for cond, _ in links)
    pl.semaphore_wait(barrier, peers)

    sent = []

    def send(cond, src, dst, ssem, rsem, to):
        def make():
            return pltpu.make_async_remote_copy(src_ref=src, dst_ref=dst, send_sem=ssem, recv_sem=rsem,
                                                device_id=to, device_id_type=pl.DeviceIdType.MESH)
        when(cond, lambda: make().start())
        sent.append((cond, make))

    def arrive(cond, dst, sem):
        when(cond, lambda: pltpu.make_async_copy(dst, dst, sem).wait())

    def own(u):
        return x_ref.at[u // H, pl.ds(u % H * part, part)]

    def block(u, slot):
        return g_ref.at[u // H, pl.ds(1 + u % H * part, part), slot]

    def along(cond, u, slot, src, side):
        ok, to = (up, (s, c + Y)) if side == 0 else (down, (s, c - Y))
        send(both(cond, ok), src, block(u, slot), vsend.at[u, side, slot], vrecv.at[u, slot], to)

    def across(cond, u, slot, src):
        for j, peer in enumerate(ypeer):
            send(cond, src, block(u, slot), ysend.at[u, j, slot], vrecv.at[u, slot], (s, peer))

    def landed(cond, u, slot):
        arrive(cond, block(u, slot), vrecv.at[u, slot])

    def rim(cond, u, slot, first=None, last=None):
        v = u // H
        if u % H == H - 1:
            last = g_ref.at[v, planes, slot] if last is None else last
            send(both(cond, s < S - 1), last, g_ref.at[v, 0, slot], hsend.at[v, 0, slot], hrecv.at[v, 0, slot],
                 (s + 1, c))
        if u % H == 0:
            first = g_ref.at[v, 1, slot] if first is None else first
            send(both(cond, s > 0), first, g_ref.at[v, planes + 1, slot], hsend.at[v, 1, slot], hrecv.at[v, 1, slot],
                 (s - 1, c))

    for u in range(units):
        for side in range(2):
            along(None, u, c, own(u), side)
        across(None, u, c, own(u))
        if u == H - 1:
            for cond, to, j, k in targets:
                send(cond, p_ref.at[j], wg_ref.at[c], psend.at[k], precv.at[c], to)
    for j in range(1, S // 2):
        send(None, w_ref, wf_ref.at[s], wsend.at[j], wrecv.at[s], (lax.rem(s + 2 * j, S), c))
    send(None, w_ref, wf_ref.at[s], wsend.at[0], wrecv.at[s], (mate, c))
    for u in range(units):
        pltpu.make_async_copy(own(u), block(u, c), lsem.at[u]).start()
        rim(None, u, c, x_ref.at[u // H, 0], x_ref.at[u // H, planes - 1])
    pltpu.make_async_copy(w_ref, wf_ref.at[s], lsem.at[units]).start()
    home = jnp.logical_and(s == lax.div(c, r), s == host)
    when(home, lambda: pltpu.make_async_copy(p_ref.at[lax.rem(c, r)], wg_ref.at[c], precv.at[c]).start())

    for side in range(2):
        def clear(side=side):
            for v in range(2):
                row = 0 if side == 0 else planes + 1
                g_ref[v, row] = jnp.zeros(g_ref.shape[2:], g_ref.dtype)
        when(s == (0 if side == 0 else S - 1), clear)

    for k in range(1, Z):
        for u in range(units):
            for side in range(2):
                zz = z - k if side == 0 else z + k
                have = zz >= 0 if side == 0 else zz < Z
                slot = zz * Y + y
                landed(have, u, slot)
                if k < Z - 1:
                    along(have, u, slot, block(u, slot), side)
                across(have, u, slot, block(u, slot))
                rim(have, u, slot)
        if k == 1:
            for j in range(1, S // 2):
                slot = lax.rem(s + 2 * j, S)
                arrive(None, wf_ref.at[slot], wrecv.at[slot])
                send(None, wf_ref.at[slot], wf_ref.at[slot], wsend.at[S // 2 + j], wrecv.at[slot], (mate, c))
    for direct in range(2):
        for k in range(n // 2):
            slot = 2 * k + core
            have = x == k % pair if direct == 0 else x != k % pair
            piece = wg_ref.at[slot]
            arrive(have, piece, precv.at[slot])
            if direct == 0:
                for j in range(1, pair):
                    send(have, piece, piece, xsend.at[j, k], precv.at[slot], (lax.rem(s + 2 * j, S), c))
            send(have, piece, piece, fsend.at[k], precv.at[slot], (mate, c))
    for k in range(Z):
        for u in range(units):
            for peer in ypeer:
                for side in range(2 if k else 1):
                    zz = z - k if side == 0 else z + k
                    have = None if k == 0 else zz >= 0 if side == 0 else zz < Z
                    slot = zz * Y + peer - z * Y
                    landed(have, u, slot)
                    rim(have, u, slot)
    for u in range(units):
        pltpu.make_async_copy(own(u), block(u, c), lsem.at[u]).wait()
    pltpu.make_async_copy(w_ref, wf_ref.at[s], lsem.at[units]).wait()
    for j in range(S // 2):
        slot = lax.rem(mate + 2 * j, S)
        arrive(None, wf_ref.at[slot], wrecv.at[slot])
    for k in range(n // 2):
        slot = 2 * k + 1 - core
        arrive(None, wg_ref.at[slot], precv.at[slot])
    for v in range(2):
        for slot in range(n):
            arrive(s > 0, g_ref.at[v, 0, slot], hrecv.at[v, 0, slot])
            arrive(s < S - 1, g_ref.at[v, planes + 1, slot], hrecv.at[v, 1, slot])
    for cond, make in sent:
        when(cond, lambda make=make: make().wait_send())


def conv_kernel(g_ref, wf_ref, wg_ref, o_ref, k_ref):
    S, _, lc, width = wf_ref.shape
    n = wg_ref.shape[0]
    planes = o_ref.shape[1]
    cells = o_ref.shape[3]
    pack = LANES // lc
    for t in range(TAPS):
        rows = pl.ds(t * lc, lc)
        k_ref[0, rows, :] = jnp.concatenate([wf_ref[i, t] for i in range(S)], axis=-1)
        f = TAPS - 1 - t
        at = (f % pack) * lc
        k_ref[1, rows, :] = jnp.concatenate([wg_ref[i, f // pack][:, at:at + lc] for i in range(n)], axis=-1)
    lane = lax.broadcasted_iota(jnp.int32, (lc, cells), 1)
    row, col = lane // COLS, lane % COLS
    nine = 9 * lc

    def step(k, carry):
        v, d = k // planes, k % planes
        total = None
        for a in range(3):
            part = jnp.dot(k_ref[v, pl.ds(a * nine, nine), :], g_ref[v, d + a], preferred_element_type=jnp.float32)
            total = part if total is None else total + part
        result = None
        for b in range(3):
            lines = None
            for c in range(3):
                at = (3 * b + c) * lc
                piece = total[at:at + lc]
                if c != 1:
                    piece = pltpu.roll(piece, (1 - c) % cells, 1)
                    piece = jnp.where(col == (0 if c == 0 else COLS - 1), 0.0, piece)
                lines = piece if lines is None else lines + piece
            if b != 1:
                lines = pltpu.roll(lines, ((1 - b) * COLS) % cells, 1)
                lines = jnp.where(row == (0 if b == 0 else ROWS - 1), 0.0, lines)
            result = lines if result is None else result + lines
        o_ref[v, d] = result.astype(o_ref.dtype)
        return carry

    lax.fori_loop(0, 2 * planes, step, 0)


def general(S, n, inputs, weights, cotangent):
    lc, planes, cells = inputs.shape
    wide = weights.shape[2]
    r = wide // lc
    C = n * lc
    Y = max(d for d in range(1, n + 1) if n % d == 0 and 2 * d * d <= n)
    Z = n // Y
    volumes = jnp.stack((inputs, cotangent)).transpose(0, 2, 1, 3)
    pack = LANES // lc
    nt = -(-TAPS // pack)
    padded = jnp.pad(weights, ((0, nt * pack - TAPS), (0, 0), (0, 0)))
    pieces = padded.reshape(nt, pack, lc, r, lc).transpose(3, 0, 4, 1, 2).reshape(r, nt, lc, pack * lc)
    vmem = pl.BlockSpec(memory_space=pltpu.VMEM)
    anyspace = pl.BlockSpec(memory_space=pl.ANY)
    dma = pltpu.SemaphoreType.DMA
    bf16 = jnp.bfloat16
    gathered, wf, wg = pl.pallas_call(
        functools.partial(gather_kernel, S, Z, Y, r),
        out_shape=(jax.ShapeDtypeStruct((2, planes + 2, n, lc, cells), bf16),
                   jax.ShapeDtypeStruct((S,) + weights.shape, bf16),
                   jax.ShapeDtypeStruct((n,) + pieces.shape[1:], bf16)),
        in_specs=[anyspace] * 3,
        out_specs=(vmem,) * 3,
        scratch_shapes=[dma((2 * H + 1,)), dma((2 * H, 2, n)), dma((2 * H, Y - 1, n)), dma((2 * H, n)), dma((2, 2, n)), dma((2, 2, n)),
                        dma((S,)), dma((S,)), dma((r,)), dma((n // 2,)), dma((S // 2, n // 2)), dma((n,))],
        compiler_params=pltpu.CompilerParams(collective_id=0, has_side_effects=True, vmem_limit_bytes=40 << 20),
        name="gather",
    )(volumes, weights, pieces)
    out = pl.pallas_call(
        conv_kernel,
        out_shape=jax.ShapeDtypeStruct((2, planes, lc, cells), bf16),
        in_specs=[vmem] * 3,
        out_specs=vmem,
        scratch_shapes=[pltpu.VMEM((2, TAPS * lc, C), bf16)],
        compiler_params=pltpu.CompilerParams(vmem_limit_bytes=48 << 20),
        name="conv",
    )(gathered.reshape(2, planes + 2, C, cells), wf, wg)
    out = out.transpose(0, 2, 1, 3)
    return out[0], out[1]


def ranges(planes):
    return [(planes - 1, 1)] + [(p, 2) for p in range(0, planes - 2, 2)] + [(planes - 2, 1)]


def split_kernel(x_ref, w_ref, out_ref, g_ref, wst_ref, stage_ref, k_ref, ob_ref,
                 asend, arecv, ysend, hsend, hrecv, wsend, wrecv, srecv, osend, orecv):
    planes, n = ob_ref.shape[0], g_ref.shape[1]
    lc, cells = g_ref.shape[2:]
    C = n * lc
    wide = w_ref.shape[2]
    chunks = ranges(planes)
    s, c = lax.axis_index("slab"), lax.axis_index("chan")
    z, y = lax.div(c, 2), lax.rem(c, 2)
    x, core = lax.div(s, 2), lax.rem(s, 2)
    h = lax.div(z, 2)
    part = TAPS // PIECES
    outer = lax.rem(z, 3) == 0
    inner = jnp.logical_not(outer)
    odd = lax.rem(z + y, 2) == 1
    even = jnp.logical_not(odd)
    b = z - 2 * h
    zp = 4 * h + 1 - z
    v = jnp.where(outer, 0, 1)
    mate, xpeer = s + 1 - 2 * core, s + 2 - 4 * x
    ypeer = 2 * z + 1 - y
    MESH = pl.DeviceIdType.MESH

    ring = [lax.rem(z + j, 4) for j in range(1, 4)]
    near, same = x == h, core == y
    other = jnp.logical_not(same)
    home_w = jnp.logical_and(inner, near)
    cross_w = jnp.logical_and(inner, jnp.logical_not(near))
    swap = (mate, ypeer)
    diag = (3 - s, ypeer)

    links = [(None, (mate, c)), (None, (xpeer, c)), (None, (s, ypeer))]
    links += [(None, (s, 2 * zz + y)) for zz in ring]
    links += [(x != core, (3 - s, c)), (odd, (s, 2 * zp + 1 - y))]
    links += [(jnp.logical_and(other, jnp.logical_or(outer, near)), swap), (jnp.logical_and(other, inner), diag)]
    barrier = pltpu.get_barrier_semaphore()
    for cond, peer in links:
        when(cond, functools.partial(pl.semaphore_signal, barrier, inc=1, device_id=peer, device_id_type=MESH))
    pl.semaphore_wait(barrier, sum(1 if cond is None else cond.astype(jnp.int32) for cond, _ in links))

    sent = []

    def send(cond, src, dst, ssem, rsem, to):
        def make():
            return pltpu.make_async_remote_copy(src_ref=src, dst_ref=dst, send_sem=ssem, recv_sem=rsem,
                                                device_id=to, device_id_type=MESH)
        when(cond, lambda: make().start())
        sent.append((cond, make))

    def local(cond, src, dst, sem):
        when(cond, lambda: pltpu.make_async_copy(src, dst, sem).start())

    def arrive(cond, dst, sem):
        when(cond, lambda: pltpu.make_async_copy(dst, dst, sem).wait())

    def piece(ref, i):
        return ref.at[pl.ds(i * part, part)]

    def shard(p, q, i):
        return wst_ref.at[p, pl.ds(i * part, part), pl.ds(pl.multiple_of(q * lc, lc), lc)]

    def block(i, slot):
        return g_ref.at[pl.ds(1 + chunks[i][0], chunks[i][1]), slot]

    def own(u, i):
        return x_ref.at[u, pl.ds(*chunks[i])]

    through = (s, 2 * jnp.where(outer, 1 + x, 3 - z) + y)
    for i in range(PIECES):
        mine = piece(w_ref, i)
        for m, (cond, dst, sem, to) in enumerate((
                (jnp.logical_and(outer, same), shard(z, core, i), wrecv.at[z, core, i], through),
                (jnp.logical_and(outer, other), piece(stage_ref, i), srecv.at[i], swap),
                (jnp.logical_and(home_w, other), shard(z, 1 - core, i), wrecv.at[z, 1 - core, i], swap),
                (jnp.logical_and(cross_w, same), piece(stage_ref, i), srecv.at[i], (xpeer, c)),
                (jnp.logical_and(cross_w, other), piece(stage_ref, i), srecv.at[i], diag))):
            send(cond, mine, dst, wsend.at[0, i], sem, to)
        local(jnp.logical_and(home_w, same), mine, shard(z, core, i), wrecv.at[z, core, i])
        local(outer, mine, shard(s, b, i), wrecv.at[s, b, i])
    for i in range(PIECES):
        mine = piece(w_ref, i)
        send(inner, mine, shard(s, b, i), wsend.at[1, i], wrecv.at[s, b, i], (s, 2 * zp + y))
        send(outer, mine, shard(s, b, i), wsend.at[2, i], wrecv.at[s, b, i], (xpeer, c))
        send(outer, mine, shard(s, b, i), wsend.at[3, i], wrecv.at[s, b, i], (mate, c))

    def depart(i):
        for zz in ring:
            send(None, own(jnp.where(lax.rem(zz, 3) == 0, 0, 1), i), block(i, c), asend.at[i, zz], arecv.at[i, c],
                 (s, 2 * zz + y))
        send(None, own(v, i), block(i, c), ysend.at[i, z], arecv.at[i, c], (s, ypeer))
        local(None, own(v, i), block(i, c), arecv.at[i, c])

    def clear():
        for edge in range(2):
            def zero(edge=edge):
                row = 0 if edge == 0 else planes + 1
                g_ref[row] = jnp.zeros(g_ref.shape[1:], g_ref.dtype)
            when(s == (0 if edge == 0 else 3), zero)

    def rim(i, slot):
        first, count = chunks[i]
        if first + count == planes:
            send(s < 3, g_ref.at[planes, slot], g_ref.at[0, slot], hsend.at[0, slot], hrecv.at[0, slot], (s + 1, c))
        if first == 0:
            send(s > 0, g_ref.at[1, slot], g_ref.at[planes + 1, slot], hsend.at[1, slot], hrecv.at[1, slot],
                 (s - 1, c))

    def column(i):
        for j, zz in enumerate([z, *ring]):
            slot = 2 * zz + y
            arrive(None, block(i, slot), arecv.at[i, slot])
            if j:
                send(None, block(i, slot), block(i, slot), ysend.at[i, zz], arecv.at[i, slot], (s, ypeer))
            rim(i, slot)

    def across(i):
        for zz in [z, *ring]:
            slot = 2 * zz + 1 - y
            arrive(None, block(i, slot), arecv.at[i, slot])
            rim(i, slot)

    def order(near_z, far_z, out):
        return jnp.where(outer, out, jnp.where(near, near_z, far_z))

    pairs = [order(z, z, s), order(3 * h, 3 - z, mate), order(3 - 3 * h, 3 * h, xpeer), order(3 - z, 3 - 3 * h, 3 - s)]
    first = [(jnp.where(outer, s if j < 2 else xpeer, pairs[j]), jnp.where(outer, b if j % 2 == 0 else 1 - b, core))
             for j in range(4)]
    second = [(jnp.where(outer, mate if j < 2 else 3 - s, pairs[j]),
               jnp.where(outer, b if j % 2 == 0 else 1 - b, 1 - core)) for j in range(4)]

    def weights(j, pieces=range(PIECES), cond=None):
        p, q = first[j]
        for i in pieces:
            ref, sem = shard(p, q, i), wrecv.at[p, q, i]
            arrive(cond, ref, sem)
            if j < 3:
                send(both(cond, None if j == 1 else home_w), ref, ref, wsend.at[5 + j, i], sem, (xpeer, c))
            send(both(cond, None if j else inner), ref, ref, wsend.at[8 + j, i], sem, (mate, c))

    def fetched(j):
        p, q = second[j]
        for i in range(PIECES):
            arrive(None, shard(p, q, i), wrecv.at[p, q, i])

    def forward(i):
        relay = jnp.where(outer, other, near)
        arrive(relay, piece(stage_ref, i), srecv.at[i])
        send(relay, piece(stage_ref, i), shard(z, core, i), wsend.at[4, i], wrecv.at[z, core, i], through)

    def build(k):
        p = pairs[k]
        for a in range(3):
            cols = pl.ds((3 * (k % 2) + a) * 2 * lc, 2 * lc)

            def tap(t, carry, a=a, cols=cols):
                rows = pl.ds(pl.multiple_of(t * 2 * lc, 2 * lc), 2 * lc)

                def plain():
                    k_ref[k // 2, rows, cols] = wst_ref[p, 9 * a + t]

                def turned():
                    k_ref[k // 2, rows, cols] = wst_ref[p, TAPS - 1 - 9 * a - t].T
                pl.when(outer)(plain)
                pl.when(inner)(turned)
                return carry
            lax.fori_loop(0, 9, tap, 0)

    lane = lax.broadcasted_iota(jnp.int32, (2 * lc, cells), 1)
    row, col = lane // COLS, lane % COLS

    def product(half, d):
        parts = [g_ref[pl.ds(d, 3), pl.ds(2 * p, 2)].reshape(6 * lc, cells) for p in pairs[2 * half:2 * half + 2]]
        return jnp.dot(k_ref[half], jnp.concatenate(parts, axis=0), preferred_element_type=jnp.float32)

    def gathered(total):
        result = None
        for t in range(3):
            lines = None
            for u in range(3):
                at = (3 * t + u) * 2 * lc
                piece = total[at:at + 2 * lc]
                if u != 1:
                    piece = pltpu.roll(piece, (1 - u) % cells, 1)
                    piece = jnp.where(col == (0 if u == 0 else COLS - 1), 0.0, piece)
                lines = piece if lines is None else lines + piece
            if t != 1:
                lines = pltpu.roll(lines, ((1 - t) * COLS) % cells, 1)
                lines = jnp.where(row == (0 if t == 0 else ROWS - 1), 0.0, lines)
            result = lines if result is None else result + lines
        return result

    home = z == 2 * h + y

    def parcel(d, q):
        stay = jnp.where(outer, b == q, jnp.logical_and(home, y == q))
        to = (s, jnp.where(outer, 2 * (2 * h + q) + y, 2 * (2 * h + y) + q))
        return stay, pltpu.make_async_remote_copy(
            src_ref=ob_ref.at[d, q], dst_ref=out_ref.at[v, d], send_sem=osend.at[d, q], recv_sem=orecv.at[v, d],
            device_id=to, device_id_type=MESH)

    def deliver(d, result):
        ob_ref[d] = result.reshape(2, lc, cells).astype(ob_ref.dtype)
        for q in range(2):
            stay, copy = parcel(d, q)
            when(jnp.logical_not(stay), copy.start)
            local(stay, ob_ref.at[d, q], out_ref.at[v, d], orecv.at[v, d])

    def loop(lo, hi, step):
        def one(d, carry):
            step(d)
            return carry
        lax.fori_loop(lo, hi, one, 0)

    def run(lo, hi):
        loop(lo, hi, lambda d: deliver(d, gathered(product(0, d) + product(1, d))))

    def halos():
        for edge in range(2):
            for slot in range(n):
                arrive((s > 0) if edge == 0 else (s < 3), g_ref.at[0 if edge == 0 else planes + 1, slot],
                       hrecv.at[edge, slot])

    depart(0)
    depart(1)
    clear()
    weights(0)
    forward(0)
    weights(1, [0])
    forward(1)
    weights(1, [1])
    forward(2)
    weights(1, [2])
    depart(2)
    weights(2, cond=home_w)
    column(0)
    column(1)
    depart(3)
    fetched(0)
    fetched(1)
    build(0)
    build(1)
    weights(2, cond=jnp.logical_not(home_w))
    across(0)
    across(1)
    column(2)
    depart(4)
    fetched(2)
    weights(3)
    column(3)
    build(2)
    across(2)
    column(4)
    fetched(3)
    build(3)
    halos()
    run(0, 3)
    across(3)
    run(3, 5)
    across(4)
    run(5, planes)
    for d in range(planes):
        for u in range(2):
            arrive(None, out_ref.at[u, d], orecv.at[u, d])
        for q in range(2):
            stay, copy = parcel(d, q)
            when(jnp.logical_not(stay), copy.wait_send)
    for cond, make in sent:
        when(cond, lambda make=make: make().wait_send())


def split(n, inputs, weights, cotangent):
    lc, planes, cells = inputs.shape
    volumes = jnp.stack((inputs, cotangent)).transpose(0, 2, 1, 3)
    dma = pltpu.SemaphoreType.DMA
    bf16 = jnp.bfloat16
    count = len(ranges(planes))
    out = pl.pallas_call(
        split_kernel,
        out_shape=jax.ShapeDtypeStruct((2, planes, lc, cells), bf16),
        in_specs=[pl.BlockSpec(memory_space=pl.ANY)] * 2,
        out_specs=pl.BlockSpec(memory_space=pltpu.VMEM),
        scratch_shapes=[pltpu.VMEM((planes + 2, n, lc, cells), bf16),
                        pltpu.VMEM((n // 2, TAPS, 2 * lc, weights.shape[2]), bf16),
                        pltpu.VMEM(weights.shape, bf16),
                        pltpu.VMEM((2, 9 * 2 * lc, 3 * n * lc // 2), bf16),
                        pltpu.VMEM((planes, 2, lc, cells), bf16),
                        dma((count, 4)), dma((count, n)), dma((count, 4)), dma((2, n)), dma((2, n)),
                        dma((12, PIECES)), dma((n // 2, 2, PIECES)), dma((PIECES,)), dma((planes, 2)), dma((2, planes))],
        compiler_params=pltpu.CompilerParams(collective_id=1, has_side_effects=True, vmem_limit_bytes=48 << 20),
        name="split",
    )(volumes, weights)
    out = out.transpose(0, 2, 1, 3)
    return out[0], out[1]


def body(S, n, inputs, weights, cotangent):
    lc = inputs.shape[0]
    if (S, n) == (4, 8) and weights.shape[2] == 2 * lc == LANES and inputs.shape[1] == 8:
        return split(n, inputs, weights, cotangent)
    return general(S, n, inputs, weights, cotangent)


def solution(mesh):
    S, n = mesh.shape["slab"], mesh.shape["chan"]
    return jax.shard_map(
        functools.partial(body, S, n),
        mesh=mesh,
        in_specs=(P("chan", "slab", None), P(None, "chan", "slab"), P("chan", "slab", None)),
        out_specs=(P("chan", "slab", None), P("chan", "slab", None)),
        check_vma=False,
    )
```

```python
import functools

import jax
import jax.numpy as jnp
from jax import lax
from jax.experimental import pallas as pl
from jax.experimental.pallas import tpu as pltpu
from jax.sharding import PartitionSpec as P

ROWS = 8
COLS = 32
TAPS = 27
LANES = 128
H = 2
PIECES = 3


def when(cond, fn):
    if cond is None:
        fn()
    else:
        pl.when(cond)(fn)


def both(a, b):
    return b if a is None else a if b is None else jnp.logical_and(a, b)


def gather_kernel(S, Z, Y, r, x_ref, w_ref, p_ref, g_ref, wf_ref, wg_ref,
                  lsem, vsend, ysend, vrecv, hsend, hrecv, wsend, wrecv, psend, fsend, xsend, precv):
    n = Z * Y
    planes = x_ref.shape[1]
    units, part = 2 * H, planes // H
    s, c = lax.axis_index("slab"), lax.axis_index("chan")
    z, y = lax.div(c, Y), lax.rem(c, Y)
    core = lax.rem(s, 2)
    mate = s + 1 - 2 * core
    ypeer = [z * Y + lax.rem(y + j, Y) for j in range(1, Y)]
    up, down = z < Z - 1, z > 0

    barrier = pltpu.get_barrier_semaphore()
    links = [(up, (s, c + Y)), (down, (s, c - Y))]
    links += [(None, (s, peer)) for peer in ypeer]
    links += [(None, (lax.rem(s + j, S), c)) for j in range(1, S)]
    targets = []
    pair = S // 2
    x = lax.div(s, 2)
    host = 2 * lax.rem(lax.div(c, 2), pair) + lax.rem(c, 2)
    for j in range(r):
        to = (host, s * r + j)
        targets.append((jnp.logical_or(to[0] != s, to[1] != c), to, j, j))
    sources = []
    for k in range(n // 2):
        frm = (lax.div(c, r), 2 * k + core)
        other = jnp.logical_or(frm[0] != s, frm[1] != c)
        sources.append((jnp.logical_and(other, x == k % pair), frm))
    links += [(t[0], t[1]) for t in targets] + sources
    for cond, peer in links:
        when(cond, functools.partial(pl.semaphore_signal, barrier, inc=1, device_id=peer,
                                     device_id_type=pl.DeviceIdType.MESH))
    peers = sum(1 if cond is None else cond.astype(jnp.int32) for cond, _ in links)
    pl.semaphore_wait(barrier, peers)

    sent = []

    def send(cond, src, dst, ssem, rsem, to):
        def make():
            return pltpu.make_async_remote_copy(src_ref=src, dst_ref=dst, send_sem=ssem, recv_sem=rsem,
                                                device_id=to, device_id_type=pl.DeviceIdType.MESH)
        when(cond, lambda: make().start())
        sent.append((cond, make))

    def arrive(cond, dst, sem):
        when(cond, lambda: pltpu.make_async_copy(dst, dst, sem).wait())

    def own(u):
        return x_ref.at[u // H, pl.ds(u % H * part, part)]

    def block(u, slot):
        return g_ref.at[u // H, pl.ds(1 + u % H * part, part), slot]

    def along(cond, u, slot, src, side):
        ok, to = (up, (s, c + Y)) if side == 0 else (down, (s, c - Y))
        send(both(cond, ok), src, block(u, slot), vsend.at[u, side, slot], vrecv.at[u, slot], to)

    def across(cond, u, slot, src):
        for j, peer in enumerate(ypeer):
            send(cond, src, block(u, slot), ysend.at[u, j, slot], vrecv.at[u, slot], (s, peer))

    def landed(cond, u, slot):
        arrive(cond, block(u, slot), vrecv.at[u, slot])

    def rim(cond, u, slot, first=None, last=None):
        v = u // H
        if u % H == H - 1:
            last = g_ref.at[v, planes, slot] if last is None else last
            send(both(cond, s < S - 1), last, g_ref.at[v, 0, slot], hsend.at[v, 0, slot], hrecv.at[v, 0, slot],
                 (s + 1, c))
        if u % H == 0:
            first = g_ref.at[v, 1, slot] if first is None else first
            send(both(cond, s > 0), first, g_ref.at[v, planes + 1, slot], hsend.at[v, 1, slot], hrecv.at[v, 1, slot],
                 (s - 1, c))

    for u in range(units):
        for side in range(2):
            along(None, u, c, own(u), side)
        across(None, u, c, own(u))
        if u == H - 1:
            for cond, to, j, k in targets:
                send(cond, p_ref.at[j], wg_ref.at[c], psend.at[k], precv.at[c], to)
    for j in range(1, S // 2):
        send(None, w_ref, wf_ref.at[s], wsend.at[j], wrecv.at[s], (lax.rem(s + 2 * j, S), c))
    send(None, w_ref, wf_ref.at[s], wsend.at[0], wrecv.at[s], (mate, c))
    for u in range(units):
        pltpu.make_async_copy(own(u), block(u, c), lsem.at[u]).start()
        rim(None, u, c, x_ref.at[u // H, 0], x_ref.at[u // H, planes - 1])
    pltpu.make_async_copy(w_ref, wf_ref.at[s], lsem.at[units]).start()
    home = jnp.logical_and(s == lax.div(c, r), s == host)
    when(home, lambda: pltpu.make_async_copy(p_ref.at[lax.rem(c, r)], wg_ref.at[c], precv.at[c]).start())

    for side in range(2):
        def clear(side=side):
            for v in range(2):
                row = 0 if side == 0 else planes + 1
                g_ref[v, row] = jnp.zeros(g_ref.shape[2:], g_ref.dtype)
        when(s == (0 if side == 0 else S - 1), clear)

    for k in range(1, Z):
        for u in range(units):
            for side in range(2):
                zz = z - k if side == 0 else z + k
                have = zz >= 0 if side == 0 else zz < Z
                slot = zz * Y + y
                landed(have, u, slot)
                if k < Z - 1:
                    along(have, u, slot, block(u, slot), side)
                across(have, u, slot, block(u, slot))
                rim(have, u, slot)
        if k == 1:
            for j in range(1, S // 2):
                slot = lax.rem(s + 2 * j, S)
                arrive(None, wf_ref.at[slot], wrecv.at[slot])
                send(None, wf_ref.at[slot], wf_ref.at[slot], wsend.at[S // 2 + j], wrecv.at[slot], (mate, c))
    for direct in range(2):
        for k in range(n // 2):
            slot = 2 * k + core
            have = x == k % pair if direct == 0 else x != k % pair
            piece = wg_ref.at[slot]
            arrive(have, piece, precv.at[slot])
            if direct == 0:
                for j in range(1, pair):
                    send(have, piece, piece, xsend.at[j, k], precv.at[slot], (lax.rem(s + 2 * j, S), c))
            send(have, piece, piece, fsend.at[k], precv.at[slot], (mate, c))
    for k in range(Z):
        for u in range(units):
            for peer in ypeer:
                for side in range(2 if k else 1):
                    zz = z - k if side == 0 else z + k
                    have = None if k == 0 else zz >= 0 if side == 0 else zz < Z
                    slot = zz * Y + peer - z * Y
                    landed(have, u, slot)
                    rim(have, u, slot)
    for u in range(units):
        pltpu.make_async_copy(own(u), block(u, c), lsem.at[u]).wait()
    pltpu.make_async_copy(w_ref, wf_ref.at[s], lsem.at[units]).wait()
    for j in range(S // 2):
        slot = lax.rem(mate + 2 * j, S)
        arrive(None, wf_ref.at[slot], wrecv.at[slot])
    for k in range(n // 2):
        slot = 2 * k + 1 - core
        arrive(None, wg_ref.at[slot], precv.at[slot])
    for v in range(2):
        for slot in range(n):
            arrive(s > 0, g_ref.at[v, 0, slot], hrecv.at[v, 0, slot])
            arrive(s < S - 1, g_ref.at[v, planes + 1, slot], hrecv.at[v, 1, slot])
    for cond, make in sent:
        when(cond, lambda make=make: make().wait_send())


def conv_kernel(g_ref, wf_ref, wg_ref, o_ref, k_ref):
    S, _, lc, width = wf_ref.shape
    n = wg_ref.shape[0]
    planes = o_ref.shape[1]
    cells = o_ref.shape[3]
    pack = LANES // lc
    for t in range(TAPS):
        rows = pl.ds(t * lc, lc)
        k_ref[0, rows, :] = jnp.concatenate([wf_ref[i, t] for i in range(S)], axis=-1)
        f = TAPS - 1 - t
        at = (f % pack) * lc
        k_ref[1, rows, :] = jnp.concatenate([wg_ref[i, f // pack][:, at:at + lc] for i in range(n)], axis=-1)
    lane = lax.broadcasted_iota(jnp.int32, (lc, cells), 1)
    row, col = lane // COLS, lane % COLS
    nine = 9 * lc

    def step(k, carry):
        v, d = k // planes, k % planes
        total = None
        for a in range(3):
            part = jnp.dot(k_ref[v, pl.ds(a * nine, nine), :], g_ref[v, d + a], preferred_element_type=jnp.float32)
            total = part if total is None else total + part
        result = None
        for b in range(3):
            lines = None
            for c in range(3):
                at = (3 * b + c) * lc
                piece = total[at:at + lc]
                if c != 1:
                    piece = pltpu.roll(piece, (1 - c) % cells, 1)
                    piece = jnp.where(col == (0 if c == 0 else COLS - 1), 0.0, piece)
                lines = piece if lines is None else lines + piece
            if b != 1:
                lines = pltpu.roll(lines, ((1 - b) * COLS) % cells, 1)
                lines = jnp.where(row == (0 if b == 0 else ROWS - 1), 0.0, lines)
            result = lines if result is None else result + lines
        o_ref[v, d] = result.astype(o_ref.dtype)
        return carry

    lax.fori_loop(0, 2 * planes, step, 0)


def general(S, n, inputs, weights, cotangent):
    lc, planes, cells = inputs.shape
    wide = weights.shape[2]
    r = wide // lc
    C = n * lc
    Y = max(d for d in range(1, n + 1) if n % d == 0 and 2 * d * d <= n)
    Z = n // Y
    volumes = jnp.stack((inputs, cotangent)).transpose(0, 2, 1, 3)
    pack = LANES // lc
    nt = -(-TAPS // pack)
    padded = jnp.pad(weights, ((0, nt * pack - TAPS), (0, 0), (0, 0)))
    pieces = padded.reshape(nt, pack, lc, r, lc).transpose(3, 0, 4, 1, 2).reshape(r, nt, lc, pack * lc)
    vmem = pl.BlockSpec(memory_space=pltpu.VMEM)
    anyspace = pl.BlockSpec(memory_space=pl.ANY)
    dma = pltpu.SemaphoreType.DMA
    bf16 = jnp.bfloat16
    gathered, wf, wg = pl.pallas_call(
        functools.partial(gather_kernel, S, Z, Y, r),
        out_shape=(jax.ShapeDtypeStruct((2, planes + 2, n, lc, cells), bf16),
                   jax.ShapeDtypeStruct((S,) + weights.shape, bf16),
                   jax.ShapeDtypeStruct((n,) + pieces.shape[1:], bf16)),
        in_specs=[anyspace] * 3,
        out_specs=(vmem,) * 3,
        scratch_shapes=[dma((2 * H + 1,)), dma((2 * H, 2, n)), dma((2 * H, Y - 1, n)), dma((2 * H, n)), dma((2, 2, n)), dma((2, 2, n)),
                        dma((S,)), dma((S,)), dma((r,)), dma((n // 2,)), dma((S // 2, n // 2)), dma((n,))],
        compiler_params=pltpu.CompilerParams(collective_id=0, has_side_effects=True, vmem_limit_bytes=40 << 20),
        name="gather",
    )(volumes, weights, pieces)
    out = pl.pallas_call(
        conv_kernel,
        out_shape=jax.ShapeDtypeStruct((2, planes, lc, cells), bf16),
        in_specs=[vmem] * 3,
        out_specs=vmem,
        scratch_shapes=[pltpu.VMEM((2, TAPS * lc, C), bf16)],
        compiler_params=pltpu.CompilerParams(vmem_limit_bytes=48 << 20),
        name="conv",
    )(gathered.reshape(2, planes + 2, C, cells), wf, wg)
    out = out.transpose(0, 2, 1, 3)
    return out[0], out[1]


def ranges(planes):
    return [(planes - 1, 1)] + [(p, 2) for p in range(0, planes - 2, 2)] + [(planes - 2, 1)]


def split_kernel(x_ref, w_ref, out_ref, g_ref, wst_ref, stage_ref, k_ref, ob_ref,
                 asend, arecv, ysend, hsend, hrecv, wsend, wrecv, srecv, osend, orecv):
    planes, n = ob_ref.shape[0], g_ref.shape[1]
    lc, cells = g_ref.shape[2:]
    C = n * lc
    chunks = ranges(planes)
    s, c = lax.axis_index("slab"), lax.axis_index("chan")
    z, y = lax.div(c, 2), lax.rem(c, 2)
    x, core = lax.div(s, 2), lax.rem(s, 2)
    h = lax.div(z, 2)
    part = TAPS // PIECES
    outer = lax.rem(z, 3) == 0
    inner = jnp.logical_not(outer)
    odd = lax.rem(z + y, 2) == 1
    b = z - 2 * h
    zp = 4 * h + 1 - z
    v = jnp.where(outer, 0, 1)
    mate, xpeer = s + 1 - 2 * core, s + 2 - 4 * x
    ypeer = 2 * z + 1 - y
    MESH = pl.DeviceIdType.MESH

    ring = [lax.rem(z + j, 4) for j in range(1, 4)]
    near, same = x == h, core == y
    other = jnp.logical_not(same)
    home_w = jnp.logical_and(inner, near)
    cross_w = jnp.logical_and(inner, jnp.logical_not(near))
    swap = (mate, ypeer)
    diag = (3 - s, ypeer)

    links = [(None, (mate, c)), (None, (xpeer, c)), (None, (s, ypeer))]
    links += [(None, (s, 2 * zz + y)) for zz in ring]
    links += [(x != core, (3 - s, c)), (odd, (s, 2 * zp + 1 - y))]
    links += [(jnp.logical_and(other, jnp.logical_or(outer, near)), swap), (jnp.logical_and(other, inner), diag)]
    barrier = pltpu.get_barrier_semaphore()
    for cond, peer in links:
        when(cond, functools.partial(pl.semaphore_signal, barrier, inc=1, device_id=peer, device_id_type=MESH))
    pl.semaphore_wait(barrier, sum(1 if cond is None else cond.astype(jnp.int32) for cond, _ in links))

    sent = []

    def send(cond, src, dst, ssem, rsem, to):
        def make():
            return pltpu.make_async_remote_copy(src_ref=src, dst_ref=dst, send_sem=ssem, recv_sem=rsem,
                                                device_id=to, device_id_type=MESH)
        when(cond, lambda: make().start())
        sent.append((cond, make))

    def local(cond, src, dst, sem):
        when(cond, lambda: pltpu.make_async_copy(src, dst, sem).start())

    def arrive(cond, dst, sem):
        when(cond, lambda: pltpu.make_async_copy(dst, dst, sem).wait())

    def piece(ref, i):
        return ref.at[pl.ds(i * part, part)]

    def shard(p, q, i):
        return wst_ref.at[p, pl.ds(i * part, part), pl.ds(pl.multiple_of(q * lc, lc), lc)]

    def block(i, slot):
        return g_ref.at[pl.ds(1 + chunks[i][0], chunks[i][1]), slot]

    def own(u, i):
        return x_ref.at[u, pl.ds(*chunks[i])]

    through = (s, 2 * jnp.where(outer, 1 + x, 3 - z) + y)
    for i in range(PIECES):
        mine = piece(w_ref, i)
        for m, (cond, dst, sem, to) in enumerate((
                (jnp.logical_and(outer, same), shard(z, core, i), wrecv.at[z, core, i], through),
                (jnp.logical_and(outer, other), piece(stage_ref, i), srecv.at[i], swap),
                (jnp.logical_and(home_w, other), shard(z, 1 - core, i), wrecv.at[z, 1 - core, i], swap),
                (jnp.logical_and(cross_w, same), piece(stage_ref, i), srecv.at[i], (xpeer, c)),
                (jnp.logical_and(cross_w, other), piece(stage_ref, i), srecv.at[i], diag))):
            send(cond, mine, dst, wsend.at[0], sem, to)
        local(jnp.logical_and(home_w, same), mine, shard(z, core, i), wrecv.at[z, core, i])
        local(outer, mine, shard(s, b, i), wrecv.at[s, b, i])
    for i in range(PIECES):
        mine = piece(w_ref, i)
        send(inner, mine, shard(s, b, i), wsend.at[1], wrecv.at[s, b, i], (s, 2 * zp + y))
        send(outer, mine, shard(s, b, i), wsend.at[2], wrecv.at[s, b, i], (xpeer, c))
        send(outer, mine, shard(s, b, i), wsend.at[3], wrecv.at[s, b, i], (mate, c))

    def depart(i):
        for zz in ring:
            send(None, own(jnp.where(lax.rem(zz, 3) == 0, 0, 1), i), block(i, c), asend.at[zz], arecv.at[i, c],
                 (s, 2 * zz + y))
        send(None, own(v, i), block(i, c), ysend.at[z], arecv.at[i, c], (s, ypeer))
        local(None, own(v, i), block(i, c), arecv.at[i, c])

    def clear():
        for edge in range(2):
            def zero(edge=edge):
                row = 0 if edge == 0 else planes + 1
                g_ref[row] = jnp.zeros(g_ref.shape[1:], g_ref.dtype)
            when(s == (0 if edge == 0 else 3), zero)

    def rim(i, slot):
        first, count = chunks[i]
        if first + count == planes:
            send(s < 3, g_ref.at[planes, slot], g_ref.at[0, slot], hsend.at[0], hrecv.at[0], (s + 1, c))
        if first == 0:
            send(s > 0, g_ref.at[1, slot], g_ref.at[planes + 1, slot], hsend.at[1], hrecv.at[1],
                 (s - 1, c))

    def column(i):
        for j, zz in enumerate([z, *ring]):
            slot = 2 * zz + y
            arrive(None, block(i, slot), arecv.at[i, slot])
            if j:
                send(None, block(i, slot), block(i, slot), ysend.at[zz], arecv.at[i, slot], (s, ypeer))
            rim(i, slot)

    def across(i):
        for zz in [z, *ring]:
            slot = 2 * zz + 1 - y
            arrive(None, block(i, slot), arecv.at[i, slot])
            rim(i, slot)

    def order(near_z, far_z, out):
        return jnp.where(outer, out, jnp.where(near, near_z, far_z))

    pairs = [order(z, z, s), order(3 * h, 3 - z, mate), order(3 - 3 * h, 3 * h, xpeer), order(3 - z, 3 - 3 * h, 3 - s)]
    first = [(jnp.where(outer, s if j < 2 else xpeer, pairs[j]), jnp.where(outer, b if j % 2 == 0 else 1 - b, core))
             for j in range(4)]
    second = [(jnp.where(outer, mate if j < 2 else 3 - s, pairs[j]),
               jnp.where(outer, b if j % 2 == 0 else 1 - b, 1 - core)) for j in range(4)]

    def weights(j, pieces=range(PIECES), cond=None):
        p, q = first[j]
        for i in pieces:
            ref, sem = shard(p, q, i), wrecv.at[p, q, i]
            arrive(cond, ref, sem)
            if j < 3:
                send(both(cond, None if j == 1 else home_w), ref, ref, wsend.at[5 + j], sem, (xpeer, c))
            send(both(cond, None if j else inner), ref, ref, wsend.at[8 + j], sem, (mate, c))

    def fetched(j):
        p, q = second[j]
        for i in range(PIECES):
            arrive(None, shard(p, q, i), wrecv.at[p, q, i])

    def forward(i):
        relay = jnp.where(outer, other, near)
        arrive(relay, piece(stage_ref, i), srecv.at[i])
        send(relay, piece(stage_ref, i), shard(z, core, i), wsend.at[4], wrecv.at[z, core, i], through)

    def build(*ks):
        def tap(t, carry):
            p = pairs[ks[0]] if len(ks) == 1 else jnp.where(t < TAPS, pairs[ks[0]], pairs[ks[1]])
            t = lax.rem(t, TAPS)
            rows = pl.ds(pl.multiple_of(lax.rem(t, 9) * 2 * lc, 2 * lc), 2 * lc)
            cols = pl.ds(pl.multiple_of(lax.div(t, 9) * C + p * 2 * lc, 2 * lc), 2 * lc)

            def plain():
                k_ref[rows, cols] = wst_ref[p, t]

            def turned():
                k_ref[rows, cols] = wst_ref[p, TAPS - 1 - t].T
            pl.when(outer)(plain)
            pl.when(inner)(turned)
            return carry
        lax.fori_loop(0, TAPS * len(ks), tap, 0)

    lane = lax.broadcasted_iota(jnp.int32, (2 * lc, cells), 1)
    row, col = lane // COLS, lane % COLS

    def product(d):
        rhs = g_ref[pl.ds(d, 3)].reshape(3 * C, cells)
        return jnp.dot(k_ref[...], rhs, preferred_element_type=jnp.float32)

    def gathered(total):
        result = None
        for t in range(3):
            lines = None
            for u in range(3):
                at = (3 * t + u) * 2 * lc
                piece = total[at:at + 2 * lc]
                if u != 1:
                    piece = pltpu.roll(piece, (1 - u) % cells, 1)
                    piece = jnp.where(col == (0 if u == 0 else COLS - 1), 0.0, piece)
                lines = piece if lines is None else lines + piece
            if t != 1:
                lines = pltpu.roll(lines, ((1 - t) * COLS) % cells, 1)
                lines = jnp.where(row == (0 if t == 0 else ROWS - 1), 0.0, lines)
            result = lines if result is None else result + lines
        return result

    home = z == 2 * h + y

    def parcel(d, q):
        stay = jnp.where(outer, b == q, jnp.logical_and(home, y == q))
        to = (s, jnp.where(outer, 2 * (2 * h + q) + y, 2 * (2 * h + y) + q))
        return stay, pltpu.make_async_remote_copy(
            src_ref=ob_ref.at[d, q], dst_ref=out_ref.at[v, d], send_sem=osend.at[q], recv_sem=orecv.at[v],
            device_id=to, device_id_type=MESH)

    def deliver(d, result):
        ob_ref[d] = result.reshape(2, lc, cells).astype(ob_ref.dtype)
        for q in range(2):
            stay, copy = parcel(d, q)
            when(jnp.logical_not(stay), copy.start)
            local(stay, ob_ref.at[d, q], out_ref.at[v, d], orecv.at[v])

    def run():
        def one(d, carry):
            for i in range(3, len(chunks)):
                if i > 3:
                    pl.when(d == 1)(functools.partial(column, i))
                pl.when(d == chunks[i][0] - 1)(functools.partial(across, i))
            deliver(d, gathered(product(d)))
            return carry
        lax.fori_loop(0, planes, one, 0)

    def halos():
        arrive(s > 0, g_ref.at[0], hrecv.at[0])
        arrive(s < 3, g_ref.at[planes + 1], hrecv.at[1])

    depart(0)
    depart(1)
    clear()
    weights(0)
    forward(0)
    weights(1, [0])
    forward(1)
    weights(1, [1])
    forward(2)
    weights(1, [2])
    depart(2)
    weights(2, cond=home_w)
    column(0)
    column(1)
    depart(3)
    fetched(0)
    fetched(1)
    build(0, 1)
    weights(2, cond=jnp.logical_not(home_w))
    across(0)
    across(1)
    column(2)
    depart(4)
    fetched(2)
    weights(3)
    build(2)
    across(2)
    column(3)
    fetched(3)
    build(3)
    halos()
    run()
    for u in range(2):
        arrive(None, out_ref.at[u], orecv.at[u])
        stay, _ = parcel(0, u)
        arrive(jnp.logical_not(stay), ob_ref.at[:, u], osend.at[u])
    for zz in ring:
        arrive(None, g_ref.at[pl.ds(1, planes), 0], asend.at[zz])
    for zz in range(4):
        arrive(None, g_ref.at[pl.ds(1, planes), 0], ysend.at[zz])
    arrive(s < 3, g_ref.at[0], hsend.at[0])
    arrive(s > 0, g_ref.at[0], hsend.at[1])
    kinds = [jnp.logical_not(jnp.logical_and(home_w, same)), inner, outer, outer,
             jnp.where(outer, other, near), home_w, None, home_w, inner, None, None, None]
    for m, cond in enumerate(kinds):
        arrive(cond, stage_ref, wsend.at[m])


def split(n, inputs, weights, cotangent):
    lc, planes, cells = inputs.shape
    volumes = jnp.stack((inputs, cotangent)).transpose(0, 2, 1, 3)
    dma = pltpu.SemaphoreType.DMA
    bf16 = jnp.bfloat16
    count = len(ranges(planes))
    out = pl.pallas_call(
        split_kernel,
        out_shape=jax.ShapeDtypeStruct((2, planes, lc, cells), bf16),
        in_specs=[pl.BlockSpec(memory_space=pl.ANY), pl.BlockSpec(memory_space=pltpu.HBM)],
        out_specs=pl.BlockSpec(memory_space=pltpu.VMEM),
        scratch_shapes=[pltpu.VMEM((planes + 2, n, lc, cells), bf16),
                        pltpu.VMEM((n // 2, TAPS, 2 * lc, weights.shape[2]), bf16),
                        pltpu.VMEM(weights.shape, bf16),
                        pltpu.VMEM((9 * 2 * lc, 3 * n * lc), bf16),
                        pltpu.VMEM((planes, 2, lc, cells), bf16),
                        dma((4,)), dma((count, n)), dma((4,)), dma((2,)), dma((2,)),
                        dma((12,)), dma((n // 2, 2, PIECES)), dma((PIECES,)), dma((2,)), dma((2,))],
        compiler_params=pltpu.CompilerParams(collective_id=1, has_side_effects=True, vmem_limit_bytes=48 << 20),
        name="split",
    )(volumes, weights)
    out = out.transpose(0, 2, 1, 3)
    return out[0], out[1]


def body(S, n, inputs, weights, cotangent):
    lc = inputs.shape[0]
    if (S, n) == (4, 8) and weights.shape[2] == 2 * lc == LANES and inputs.shape[1] == 8:
        return split(n, inputs, weights, cotangent)
    return general(S, n, inputs, weights, cotangent)


def solution(mesh):
    S, n = mesh.shape["slab"], mesh.shape["chan"]
    return jax.shard_map(
        functools.partial(body, S, n),
        mesh=mesh,
        in_specs=(P("chan", "slab", None), P(None, "chan", "slab"), P("chan", "slab", None)),
        out_specs=(P("chan", "slab", None), P("chan", "slab", None)),
        check_vma=False,
    )
```

```python
import functools

import jax
import jax.numpy as jnp
from jax import lax
from jax.experimental import pallas as pl
from jax.experimental.pallas import tpu as pltpu
from jax.sharding import PartitionSpec as P

ROWS = 8
COLS = 32
TAPS = 27
LANES = 128
H = 2
PIECES = 3


def when(cond, fn):
    if cond is None:
        fn()
    else:
        pl.when(cond)(fn)


def both(a, b):
    return b if a is None else a if b is None else jnp.logical_and(a, b)


def gather_kernel(S, Z, Y, r, x_ref, w_ref, p_ref, g_ref, wf_ref, wg_ref,
                  lsem, vsend, ysend, vrecv, hsend, hrecv, wsend, wrecv, psend, fsend, xsend, precv):
    n = Z * Y
    planes = x_ref.shape[1]
    units, part = 2 * H, planes // H
    s, c = lax.axis_index("slab"), lax.axis_index("chan")
    z, y = lax.div(c, Y), lax.rem(c, Y)
    core = lax.rem(s, 2)
    mate = s + 1 - 2 * core
    ypeer = [z * Y + lax.rem(y + j, Y) for j in range(1, Y)]
    up, down = z < Z - 1, z > 0

    barrier = pltpu.get_barrier_semaphore()
    links = [(up, (s, c + Y)), (down, (s, c - Y))]
    links += [(None, (s, peer)) for peer in ypeer]
    links += [(None, (lax.rem(s + j, S), c)) for j in range(1, S)]
    targets = []
    pair = S // 2
    x = lax.div(s, 2)
    host = 2 * lax.rem(lax.div(c, 2), pair) + lax.rem(c, 2)
    for j in range(r):
        to = (host, s * r + j)
        targets.append((jnp.logical_or(to[0] != s, to[1] != c), to, j, j))
    sources = []
    for k in range(n // 2):
        frm = (lax.div(c, r), 2 * k + core)
        other = jnp.logical_or(frm[0] != s, frm[1] != c)
        sources.append((jnp.logical_and(other, x == k % pair), frm))
    links += [(t[0], t[1]) for t in targets] + sources
    for cond, peer in links:
        when(cond, functools.partial(pl.semaphore_signal, barrier, inc=1, device_id=peer,
                                     device_id_type=pl.DeviceIdType.MESH))
    peers = sum(1 if cond is None else cond.astype(jnp.int32) for cond, _ in links)
    pl.semaphore_wait(barrier, peers)

    sent = []

    def send(cond, src, dst, ssem, rsem, to):
        def make():
            return pltpu.make_async_remote_copy(src_ref=src, dst_ref=dst, send_sem=ssem, recv_sem=rsem,
                                                device_id=to, device_id_type=pl.DeviceIdType.MESH)
        when(cond, lambda: make().start())
        sent.append((cond, make))

    def arrive(cond, dst, sem):
        when(cond, lambda: pltpu.make_async_copy(dst, dst, sem).wait())

    def own(u):
        return x_ref.at[u // H, pl.ds(u % H * part, part)]

    def block(u, slot):
        return g_ref.at[u // H, pl.ds(1 + u % H * part, part), slot]

    def along(cond, u, slot, src, side):
        ok, to = (up, (s, c + Y)) if side == 0 else (down, (s, c - Y))
        send(both(cond, ok), src, block(u, slot), vsend.at[u, side, slot], vrecv.at[u, slot], to)

    def across(cond, u, slot, src):
        for j, peer in enumerate(ypeer):
            send(cond, src, block(u, slot), ysend.at[u, j, slot], vrecv.at[u, slot], (s, peer))

    def landed(cond, u, slot):
        arrive(cond, block(u, slot), vrecv.at[u, slot])

    def rim(cond, u, slot, first=None, last=None):
        v = u // H
        if u % H == H - 1:
            last = g_ref.at[v, planes, slot] if last is None else last
            send(both(cond, s < S - 1), last, g_ref.at[v, 0, slot], hsend.at[v, 0, slot], hrecv.at[v, 0, slot],
                 (s + 1, c))
        if u % H == 0:
            first = g_ref.at[v, 1, slot] if first is None else first
            send(both(cond, s > 0), first, g_ref.at[v, planes + 1, slot], hsend.at[v, 1, slot], hrecv.at[v, 1, slot],
                 (s - 1, c))

    for u in range(units):
        for side in range(2):
            along(None, u, c, own(u), side)
        across(None, u, c, own(u))
        if u == H - 1:
            for cond, to, j, k in targets:
                send(cond, p_ref.at[j], wg_ref.at[c], psend.at[k], precv.at[c], to)
    for j in range(1, S // 2):
        send(None, w_ref, wf_ref.at[s], wsend.at[j], wrecv.at[s], (lax.rem(s + 2 * j, S), c))
    send(None, w_ref, wf_ref.at[s], wsend.at[0], wrecv.at[s], (mate, c))
    for u in range(units):
        pltpu.make_async_copy(own(u), block(u, c), lsem.at[u]).start()
        rim(None, u, c, x_ref.at[u // H, 0], x_ref.at[u // H, planes - 1])
    pltpu.make_async_copy(w_ref, wf_ref.at[s], lsem.at[units]).start()
    home = jnp.logical_and(s == lax.div(c, r), s == host)
    when(home, lambda: pltpu.make_async_copy(p_ref.at[lax.rem(c, r)], wg_ref.at[c], precv.at[c]).start())

    for side in range(2):
        def clear(side=side):
            for v in range(2):
                row = 0 if side == 0 else planes + 1
                g_ref[v, row] = jnp.zeros(g_ref.shape[2:], g_ref.dtype)
        when(s == (0 if side == 0 else S - 1), clear)

    for k in range(1, Z):
        for u in range(units):
            for side in range(2):
                zz = z - k if side == 0 else z + k
                have = zz >= 0 if side == 0 else zz < Z
                slot = zz * Y + y
                landed(have, u, slot)
                if k < Z - 1:
                    along(have, u, slot, block(u, slot), side)
                across(have, u, slot, block(u, slot))
                rim(have, u, slot)
        if k == 1:
            for j in range(1, S // 2):
                slot = lax.rem(s + 2 * j, S)
                arrive(None, wf_ref.at[slot], wrecv.at[slot])
                send(None, wf_ref.at[slot], wf_ref.at[slot], wsend.at[S // 2 + j], wrecv.at[slot], (mate, c))
    for direct in range(2):
        for k in range(n // 2):
            slot = 2 * k + core
            have = x == k % pair if direct == 0 else x != k % pair
            piece = wg_ref.at[slot]
            arrive(have, piece, precv.at[slot])
            if direct == 0:
                for j in range(1, pair):
                    send(have, piece, piece, xsend.at[j, k], precv.at[slot], (lax.rem(s + 2 * j, S), c))
            send(have, piece, piece, fsend.at[k], precv.at[slot], (mate, c))
    for k in range(Z):
        for u in range(units):
            for peer in ypeer:
                for side in range(2 if k else 1):
                    zz = z - k if side == 0 else z + k
                    have = None if k == 0 else zz >= 0 if side == 0 else zz < Z
                    slot = zz * Y + peer - z * Y
                    landed(have, u, slot)
                    rim(have, u, slot)
    for u in range(units):
        pltpu.make_async_copy(own(u), block(u, c), lsem.at[u]).wait()
    pltpu.make_async_copy(w_ref, wf_ref.at[s], lsem.at[units]).wait()
    for j in range(S // 2):
        slot = lax.rem(mate + 2 * j, S)
        arrive(None, wf_ref.at[slot], wrecv.at[slot])
    for k in range(n // 2):
        slot = 2 * k + 1 - core
        arrive(None, wg_ref.at[slot], precv.at[slot])
    for v in range(2):
        for slot in range(n):
            arrive(s > 0, g_ref.at[v, 0, slot], hrecv.at[v, 0, slot])
            arrive(s < S - 1, g_ref.at[v, planes + 1, slot], hrecv.at[v, 1, slot])
    for cond, make in sent:
        when(cond, lambda make=make: make().wait_send())


def conv_kernel(g_ref, wf_ref, wg_ref, o_ref, k_ref):
    S, _, lc, width = wf_ref.shape
    n = wg_ref.shape[0]
    planes = o_ref.shape[1]
    cells = o_ref.shape[3]
    pack = LANES // lc
    for t in range(TAPS):
        rows = pl.ds(t * lc, lc)
        k_ref[0, rows, :] = jnp.concatenate([wf_ref[i, t] for i in range(S)], axis=-1)
        f = TAPS - 1 - t
        at = (f % pack) * lc
        k_ref[1, rows, :] = jnp.concatenate([wg_ref[i, f // pack][:, at:at + lc] for i in range(n)], axis=-1)
    lane = lax.broadcasted_iota(jnp.int32, (lc, cells), 1)
    row, col = lane // COLS, lane % COLS
    nine = 9 * lc

    def step(k, carry):
        v, d = k // planes, k % planes
        total = None
        for a in range(3):
            part = jnp.dot(k_ref[v, pl.ds(a * nine, nine), :], g_ref[v, d + a], preferred_element_type=jnp.float32)
            total = part if total is None else total + part
        result = None
        for b in range(3):
            lines = None
            for c in range(3):
                at = (3 * b + c) * lc
                piece = total[at:at + lc]
                if c != 1:
                    piece = pltpu.roll(piece, (1 - c) % cells, 1)
                    piece = jnp.where(col == (0 if c == 0 else COLS - 1), 0.0, piece)
                lines = piece if lines is None else lines + piece
            if b != 1:
                lines = pltpu.roll(lines, ((1 - b) * COLS) % cells, 1)
                lines = jnp.where(row == (0 if b == 0 else ROWS - 1), 0.0, lines)
            result = lines if result is None else result + lines
        o_ref[v, d] = result.astype(o_ref.dtype)
        return carry

    lax.fori_loop(0, 2 * planes, step, 0)


def general(S, n, inputs, weights, cotangent):
    lc, planes, cells = inputs.shape
    wide = weights.shape[2]
    r = wide // lc
    C = n * lc
    Y = max(d for d in range(1, n + 1) if n % d == 0 and 2 * d * d <= n)
    Z = n // Y
    volumes = jnp.stack((inputs, cotangent)).transpose(0, 2, 1, 3)
    pack = LANES // lc
    nt = -(-TAPS // pack)
    padded = jnp.pad(weights, ((0, nt * pack - TAPS), (0, 0), (0, 0)))
    pieces = padded.reshape(nt, pack, lc, r, lc).transpose(3, 0, 4, 1, 2).reshape(r, nt, lc, pack * lc)
    vmem = pl.BlockSpec(memory_space=pltpu.VMEM)
    anyspace = pl.BlockSpec(memory_space=pl.ANY)
    dma = pltpu.SemaphoreType.DMA
    bf16 = jnp.bfloat16
    gathered, wf, wg = pl.pallas_call(
        functools.partial(gather_kernel, S, Z, Y, r),
        out_shape=(jax.ShapeDtypeStruct((2, planes + 2, n, lc, cells), bf16),
                   jax.ShapeDtypeStruct((S,) + weights.shape, bf16),
                   jax.ShapeDtypeStruct((n,) + pieces.shape[1:], bf16)),
        in_specs=[anyspace] * 3,
        out_specs=(vmem,) * 3,
        scratch_shapes=[dma((2 * H + 1,)), dma((2 * H, 2, n)), dma((2 * H, Y - 1, n)), dma((2 * H, n)), dma((2, 2, n)), dma((2, 2, n)),
                        dma((S,)), dma((S,)), dma((r,)), dma((n // 2,)), dma((S // 2, n // 2)), dma((n,))],
        compiler_params=pltpu.CompilerParams(collective_id=0, has_side_effects=True, vmem_limit_bytes=40 << 20),
        name="gather",
    )(volumes, weights, pieces)
    out = pl.pallas_call(
        conv_kernel,
        out_shape=jax.ShapeDtypeStruct((2, planes, lc, cells), bf16),
        in_specs=[vmem] * 3,
        out_specs=vmem,
        scratch_shapes=[pltpu.VMEM((2, TAPS * lc, C), bf16)],
        compiler_params=pltpu.CompilerParams(vmem_limit_bytes=48 << 20),
        name="conv",
    )(gathered.reshape(2, planes + 2, C, cells), wf, wg)
    out = out.transpose(0, 2, 1, 3)
    return out[0], out[1]


def ranges(planes):
    return [(planes - 1, 1)] + [(p, 2) for p in range(0, planes - 2, 2)] + [(planes - 2, 1)]


def split_kernel(x_ref, w_ref, out_ref, g_ref, wst_ref, stage_ref, k_ref, ob_ref,
                 asend, arecv, ysend, hsend, hrecv, wsend, wrecv, srecv, osend, orecv):
    planes, n = ob_ref.shape[0], g_ref.shape[1]
    lc, cells = g_ref.shape[2:]
    C = n * lc
    chunks = ranges(planes)
    s, c = lax.axis_index("slab"), lax.axis_index("chan")
    z, y = lax.div(c, 2), lax.rem(c, 2)
    x, core = lax.div(s, 2), lax.rem(s, 2)
    h = lax.div(z, 2)
    part = TAPS // PIECES
    outer = lax.rem(z, 3) == 0
    inner = jnp.logical_not(outer)
    odd = lax.rem(z + y, 2) == 1
    b = z - 2 * h
    zp = 4 * h + 1 - z
    v = jnp.where(outer, 0, 1)
    mate, xpeer = s + 1 - 2 * core, s + 2 - 4 * x
    ypeer = 2 * z + 1 - y
    MESH = pl.DeviceIdType.MESH

    ring = [lax.rem(z + j, 4) for j in range(1, 4)]
    near, same = x == h, core == y
    other = jnp.logical_not(same)
    home_w = jnp.logical_and(inner, near)
    cross_w = jnp.logical_and(inner, jnp.logical_not(near))
    swap = (mate, ypeer)
    diag = (3 - s, ypeer)

    links = [(None, (mate, c)), (None, (xpeer, c)), (None, (s, ypeer))]
    links += [(None, (s, 2 * zz + y)) for zz in ring]
    links += [(x != core, (3 - s, c)), (odd, (s, 2 * zp + 1 - y))]
    links += [(jnp.logical_and(other, jnp.logical_or(outer, near)), swap), (jnp.logical_and(other, inner), diag)]
    barrier = pltpu.get_barrier_semaphore()
    for cond, peer in links:
        when(cond, functools.partial(pl.semaphore_signal, barrier, inc=1, device_id=peer, device_id_type=MESH))
    pl.semaphore_wait(barrier, sum(1 if cond is None else cond.astype(jnp.int32) for cond, _ in links))

    sent = []

    def send(cond, src, dst, ssem, rsem, to):
        def make():
            return pltpu.make_async_remote_copy(src_ref=src, dst_ref=dst, send_sem=ssem, recv_sem=rsem,
                                                device_id=to, device_id_type=MESH)
        when(cond, lambda: make().start())
        sent.append((cond, make))

    def local(cond, src, dst, sem):
        when(cond, lambda: pltpu.make_async_copy(src, dst, sem).start())

    def arrive(cond, dst, sem):
        when(cond, lambda: pltpu.make_async_copy(dst, dst, sem).wait())

    def piece(ref, i):
        return ref.at[pl.ds(i * part, part)]

    def shard(p, q, i):
        return wst_ref.at[p, pl.ds(i * part, part), pl.ds(pl.multiple_of(q * lc, lc), lc)]

    def block(i, slot):
        return g_ref.at[pl.ds(1 + chunks[i][0], chunks[i][1]), slot]

    def own(u, i):
        return x_ref.at[u, pl.ds(*chunks[i])]

    through = (s, 2 * jnp.where(outer, 1 + x, 3 - z) + y)
    for i in range(PIECES):
        mine = piece(w_ref, i)
        for m, (cond, dst, sem, to) in enumerate((
                (jnp.logical_and(outer, same), shard(z, core, i), wrecv.at[z, core, i], through),
                (jnp.logical_and(outer, other), piece(stage_ref, i), srecv.at[i], swap),
                (jnp.logical_and(home_w, other), shard(z, 1 - core, i), wrecv.at[z, 1 - core, i], swap),
                (jnp.logical_and(cross_w, same), piece(stage_ref, i), srecv.at[i], (xpeer, c)),
                (jnp.logical_and(cross_w, other), piece(stage_ref, i), srecv.at[i], diag))):
            send(cond, mine, dst, wsend.at[0], sem, to)
        local(jnp.logical_and(home_w, same), mine, shard(z, core, i), wrecv.at[z, core, i])
        local(outer, mine, shard(s, b, i), wrecv.at[s, b, i])
    for i in range(PIECES):
        mine = piece(w_ref, i)
        send(inner, mine, shard(s, b, i), wsend.at[1], wrecv.at[s, b, i], (s, 2 * zp + y))
        send(outer, mine, shard(s, b, i), wsend.at[2], wrecv.at[s, b, i], (xpeer, c))
        send(outer, mine, shard(s, b, i), wsend.at[3], wrecv.at[s, b, i], (mate, c))

    def depart(i):
        for zz in ring:
            send(None, own(jnp.where(lax.rem(zz, 3) == 0, 0, 1), i), block(i, c), asend.at[zz], arecv.at[i, c],
                 (s, 2 * zz + y))
        send(None, own(v, i), block(i, c), ysend.at[z], arecv.at[i, c], (s, ypeer))
        local(None, own(v, i), block(i, c), arecv.at[i, c])

    def clear():
        for edge in range(2):
            def zero(edge=edge):
                row = 0 if edge == 0 else planes + 1
                g_ref[row] = jnp.zeros(g_ref.shape[1:], g_ref.dtype)
            when(s == (0 if edge == 0 else 3), zero)

    def rim(i, slot):
        first, count = chunks[i]
        if first + count == planes:
            send(s < 3, g_ref.at[planes, slot], g_ref.at[0, slot], hsend.at[0], hrecv.at[0], (s + 1, c))
        if first == 0:
            send(s > 0, g_ref.at[1, slot], g_ref.at[planes + 1, slot], hsend.at[1], hrecv.at[1],
                 (s - 1, c))

    def column(i):
        for j, zz in enumerate([z, *ring]):
            slot = 2 * zz + y
            arrive(None, block(i, slot), arecv.at[i, slot])
            if j:
                send(None, block(i, slot), block(i, slot), ysend.at[zz], arecv.at[i, slot], (s, ypeer))
            rim(i, slot)

    def across(i):
        for zz in [z, *ring]:
            slot = 2 * zz + 1 - y
            arrive(None, block(i, slot), arecv.at[i, slot])
            rim(i, slot)

    def order(near_z, far_z, out):
        return jnp.where(outer, out, jnp.where(near, near_z, far_z))

    pairs = [order(z, z, s), order(3 * h, 3 - z, mate), order(3 - 3 * h, 3 * h, xpeer), order(3 - z, 3 - 3 * h, 3 - s)]
    first = [(jnp.where(outer, s if j < 2 else xpeer, pairs[j]), jnp.where(outer, b if j % 2 == 0 else 1 - b, core))
             for j in range(4)]
    second = [(jnp.where(outer, mate if j < 2 else 3 - s, pairs[j]),
               jnp.where(outer, b if j % 2 == 0 else 1 - b, 1 - core)) for j in range(4)]

    def weights(j, pieces=range(PIECES), cond=None):
        p, q = first[j]
        for i in pieces:
            ref, sem = shard(p, q, i), wrecv.at[p, q, i]
            arrive(cond, ref, sem)
            if j < 3:
                send(both(cond, None if j == 1 else home_w), ref, ref, wsend.at[5 + j], sem, (xpeer, c))
            send(both(cond, None if j else inner), ref, ref, wsend.at[8 + j], sem, (mate, c))

    def fetched(j):
        p, q = second[j]
        for i in range(PIECES):
            arrive(None, shard(p, q, i), wrecv.at[p, q, i])

    def forward(i):
        relay = jnp.where(outer, other, near)
        arrive(relay, piece(stage_ref, i), srecv.at[i])
        send(relay, piece(stage_ref, i), shard(z, core, i), wsend.at[4], wrecv.at[z, core, i], through)

    def build(*ks):
        def tap(t, carry):
            p = pairs[ks[0]] if len(ks) == 1 else jnp.where(t < TAPS, pairs[ks[0]], pairs[ks[1]])
            t = lax.rem(t, TAPS)
            rows = pl.ds(pl.multiple_of(lax.rem(t, 9) * 2 * lc, 2 * lc), 2 * lc)
            cols = pl.ds(pl.multiple_of(lax.div(t, 9) * C + p * 2 * lc, 2 * lc), 2 * lc)

            def plain():
                k_ref[rows, cols] = wst_ref[p, t]

            def turned():
                k_ref[rows, cols] = wst_ref[p, TAPS - 1 - t].T
            pl.when(outer)(plain)
            pl.when(inner)(turned)
            return carry
        lax.fori_loop(0, TAPS * len(ks), tap, 0)

    def finish(k):
        p, (m, q) = pairs[k], second[k]

        def tap(t, carry):
            at = jnp.where(outer, t, TAPS - 1 - t)
            rows = pl.ds(pl.multiple_of(lax.rem(at, 9) * 2 * lc, 2 * lc), 2 * lc)
            cols = pl.ds(pl.multiple_of(lax.div(at, 9) * C + p * 2 * lc, 2 * lc), 2 * lc)

            def plain():
                k_ref[rows, cols] = wst_ref[p, t]

            def turned():
                k_ref[rows, cols] = wst_ref[p, t].T
            pl.when(outer)(plain)
            pl.when(inner)(turned)
            return carry

        def step(i, carry):
            arrive(None, shard(m, q, i), wrecv.at[m, q, i])
            return lax.fori_loop(i * part, (i + 1) * part, tap, carry)
        lax.fori_loop(0, PIECES, step, 0)

    lane = lax.broadcasted_iota(jnp.int32, (2 * lc, cells), 1)
    row, col = lane // COLS, lane % COLS

    def product(d):
        rhs = g_ref[pl.ds(d, 3)].reshape(3 * C, cells)
        return jnp.dot(k_ref[...], rhs, preferred_element_type=jnp.float32)

    def gathered(total):
        result = None
        for t in range(3):
            lines = None
            for u in range(3):
                at = (3 * t + u) * 2 * lc
                piece = total[at:at + 2 * lc]
                if u != 1:
                    piece = pltpu.roll(piece, (1 - u) % cells, 1)
                    piece = jnp.where(col == (0 if u == 0 else COLS - 1), 0.0, piece)
                lines = piece if lines is None else lines + piece
            if t != 1:
                lines = pltpu.roll(lines, ((1 - t) * COLS) % cells, 1)
                lines = jnp.where(row == (0 if t == 0 else ROWS - 1), 0.0, lines)
            result = lines if result is None else result + lines
        return result

    home = z == 2 * h + y

    def parcel(d, q):
        stay = jnp.where(outer, b == q, jnp.logical_and(home, y == q))
        to = (s, jnp.where(outer, 2 * (2 * h + q) + y, 2 * (2 * h + y) + q))
        return stay, pltpu.make_async_remote_copy(
            src_ref=ob_ref.at[d, q], dst_ref=out_ref.at[v, d], send_sem=osend.at[q], recv_sem=orecv.at[v],
            device_id=to, device_id_type=MESH)

    def deliver(d, result):
        ob_ref[d] = result.reshape(2, lc, cells).astype(ob_ref.dtype)
        for q in range(2):
            stay, copy = parcel(d, q)
            when(jnp.logical_not(stay), copy.start)
            local(stay, ob_ref.at[d, q], out_ref.at[v, d], orecv.at[v])

    def run():
        def one(d, carry):
            for i in range(3, len(chunks)):
                if i > 3:
                    pl.when(d == 1)(functools.partial(column, i))
                pl.when(d == chunks[i][0] - 1)(functools.partial(across, i))
            deliver(d, gathered(product(d)))
            return carry
        lax.fori_loop(0, planes, one, 0)

    def halos():
        arrive(s > 0, g_ref.at[0], hrecv.at[0])
        arrive(s < 3, g_ref.at[planes + 1], hrecv.at[1])

    depart(0)
    depart(1)
    clear()
    weights(0)
    forward(0)
    weights(1, [0])
    forward(1)
    weights(1, [1])
    forward(2)
    weights(1, [2])
    depart(2)
    weights(2, cond=home_w)
    column(0)
    column(1)
    depart(3)
    fetched(0)
    fetched(1)
    build(0, 1)
    weights(2, cond=jnp.logical_not(home_w))
    across(0)
    across(1)
    column(2)
    depart(4)
    fetched(2)
    weights(3)
    build(2)
    across(2)
    column(3)
    finish(3)
    halos()
    run()
    for u in range(2):
        arrive(None, out_ref.at[u], orecv.at[u])
        stay, _ = parcel(0, u)
        arrive(jnp.logical_not(stay), ob_ref.at[:, u], osend.at[u])
    for zz in ring:
        arrive(None, g_ref.at[pl.ds(1, planes), 0], asend.at[zz])
    for zz in range(4):
        arrive(None, g_ref.at[pl.ds(1, planes), 0], ysend.at[zz])
    arrive(s < 3, g_ref.at[0], hsend.at[0])
    arrive(s > 0, g_ref.at[0], hsend.at[1])
    kinds = [jnp.logical_not(jnp.logical_and(home_w, same)), inner, outer, outer,
             jnp.where(outer, other, near), home_w, None, home_w, inner, None, None, None]
    for m, cond in enumerate(kinds):
        arrive(cond, stage_ref, wsend.at[m])


def split(n, inputs, weights, cotangent):
    lc, planes, cells = inputs.shape
    volumes = jnp.stack((inputs, cotangent)).transpose(0, 2, 1, 3)
    dma = pltpu.SemaphoreType.DMA
    bf16 = jnp.bfloat16
    count = len(ranges(planes))
    out = pl.pallas_call(
        split_kernel,
        out_shape=jax.ShapeDtypeStruct((2, planes, lc, cells), bf16),
        in_specs=[pl.BlockSpec(memory_space=pl.ANY), pl.BlockSpec(memory_space=pltpu.HBM)],
        out_specs=pl.BlockSpec(memory_space=pltpu.VMEM),
        scratch_shapes=[pltpu.VMEM((planes + 2, n, lc, cells), bf16),
                        pltpu.VMEM((n // 2, TAPS, 2 * lc, weights.shape[2]), bf16),
                        pltpu.VMEM(weights.shape, bf16),
                        pltpu.VMEM((9 * 2 * lc, 3 * n * lc), bf16),
                        pltpu.VMEM((planes, 2, lc, cells), bf16),
                        dma((4,)), dma((count, n)), dma((4,)), dma((2,)), dma((2,)),
                        dma((12,)), dma((n // 2, 2, PIECES)), dma((PIECES,)), dma((2,)), dma((2,))],
        compiler_params=pltpu.CompilerParams(collective_id=1, has_side_effects=True, vmem_limit_bytes=48 << 20),
        name="split",
    )(volumes, weights)
    out = out.transpose(0, 2, 1, 3)
    return out[0], out[1]


def body(S, n, inputs, weights, cotangent):
    lc = inputs.shape[0]
    if (S, n) == (4, 8) and weights.shape[2] == 2 * lc == LANES and inputs.shape[1] == 8:
        return split(n, inputs, weights, cotangent)
    return general(S, n, inputs, weights, cotangent)


def solution(mesh):
    S, n = mesh.shape["slab"], mesh.shape["chan"]
    return jax.shard_map(
        functools.partial(body, S, n),
        mesh=mesh,
        in_specs=(P("chan", "slab", None), P(None, "chan", "slab"), P("chan", "slab", None)),
        out_specs=(P("chan", "slab", None), P("chan", "slab", None)),
        check_vma=False,
    )
```

```python
import functools

import jax
import jax.numpy as jnp
from jax import lax
from jax.experimental import pallas as pl
from jax.experimental.pallas import tpu as pltpu
from jax.sharding import PartitionSpec as P

ROWS = 8
COLS = 32
TAPS = 27
LANES = 128
H = 2
PIECES = 3


def when(cond, fn):
    if cond is None:
        fn()
    else:
        pl.when(cond)(fn)


def both(a, b):
    return b if a is None else a if b is None else jnp.logical_and(a, b)


def gather_kernel(S, Z, Y, r, x_ref, w_ref, p_ref, g_ref, wf_ref, wg_ref,
                  lsem, vsend, ysend, vrecv, hsend, hrecv, wsend, wrecv, psend, fsend, xsend, precv):
    n = Z * Y
    planes = x_ref.shape[1]
    units, part = 2 * H, planes // H
    s, c = lax.axis_index("slab"), lax.axis_index("chan")
    z, y = lax.div(c, Y), lax.rem(c, Y)
    core = lax.rem(s, 2)
    mate = s + 1 - 2 * core
    ypeer = [z * Y + lax.rem(y + j, Y) for j in range(1, Y)]
    up, down = z < Z - 1, z > 0

    barrier = pltpu.get_barrier_semaphore()
    links = [(up, (s, c + Y)), (down, (s, c - Y))]
    links += [(None, (s, peer)) for peer in ypeer]
    links += [(None, (lax.rem(s + j, S), c)) for j in range(1, S)]
    targets = []
    pair = S // 2
    x = lax.div(s, 2)
    host = 2 * lax.rem(lax.div(c, 2), pair) + lax.rem(c, 2)
    for j in range(r):
        to = (host, s * r + j)
        targets.append((jnp.logical_or(to[0] != s, to[1] != c), to, j, j))
    sources = []
    for k in range(n // 2):
        frm = (lax.div(c, r), 2 * k + core)
        other = jnp.logical_or(frm[0] != s, frm[1] != c)
        sources.append((jnp.logical_and(other, x == k % pair), frm))
    links += [(t[0], t[1]) for t in targets] + sources
    for cond, peer in links:
        when(cond, functools.partial(pl.semaphore_signal, barrier, inc=1, device_id=peer,
                                     device_id_type=pl.DeviceIdType.MESH))
    peers = sum(1 if cond is None else cond.astype(jnp.int32) for cond, _ in links)
    pl.semaphore_wait(barrier, peers)

    sent = []

    def send(cond, src, dst, ssem, rsem, to):
        def make():
            return pltpu.make_async_remote_copy(src_ref=src, dst_ref=dst, send_sem=ssem, recv_sem=rsem,
                                                device_id=to, device_id_type=pl.DeviceIdType.MESH)
        when(cond, lambda: make().start())
        sent.append((cond, make))

    def arrive(cond, dst, sem):
        when(cond, lambda: pltpu.make_async_copy(dst, dst, sem).wait())

    def own(u):
        return x_ref.at[u // H, pl.ds(u % H * part, part)]

    def block(u, slot):
        return g_ref.at[u // H, pl.ds(1 + u % H * part, part), slot]

    def along(cond, u, slot, src, side):
        ok, to = (up, (s, c + Y)) if side == 0 else (down, (s, c - Y))
        send(both(cond, ok), src, block(u, slot), vsend.at[u, side, slot], vrecv.at[u, slot], to)

    def across(cond, u, slot, src):
        for j, peer in enumerate(ypeer):
            send(cond, src, block(u, slot), ysend.at[u, j, slot], vrecv.at[u, slot], (s, peer))

    def landed(cond, u, slot):
        arrive(cond, block(u, slot), vrecv.at[u, slot])

    def rim(cond, u, slot, first=None, last=None):
        v = u // H
        if u % H == H - 1:
            last = g_ref.at[v, planes, slot] if last is None else last
            send(both(cond, s < S - 1), last, g_ref.at[v, 0, slot], hsend.at[v, 0, slot], hrecv.at[v, 0, slot],
                 (s + 1, c))
        if u % H == 0:
            first = g_ref.at[v, 1, slot] if first is None else first
            send(both(cond, s > 0), first, g_ref.at[v, planes + 1, slot], hsend.at[v, 1, slot], hrecv.at[v, 1, slot],
                 (s - 1, c))

    for u in range(units):
        for side in range(2):
            along(None, u, c, own(u), side)
        across(None, u, c, own(u))
        if u == H - 1:
            for cond, to, j, k in targets:
                send(cond, p_ref.at[j], wg_ref.at[c], psend.at[k], precv.at[c], to)
    for j in range(1, S // 2):
        send(None, w_ref, wf_ref.at[s], wsend.at[j], wrecv.at[s], (lax.rem(s + 2 * j, S), c))
    send(None, w_ref, wf_ref.at[s], wsend.at[0], wrecv.at[s], (mate, c))
    for u in range(units):
        pltpu.make_async_copy(own(u), block(u, c), lsem.at[u]).start()
        rim(None, u, c, x_ref.at[u // H, 0], x_ref.at[u // H, planes - 1])
    pltpu.make_async_copy(w_ref, wf_ref.at[s], lsem.at[units]).start()
    home = jnp.logical_and(s == lax.div(c, r), s == host)
    when(home, lambda: pltpu.make_async_copy(p_ref.at[lax.rem(c, r)], wg_ref.at[c], precv.at[c]).start())

    for side in range(2):
        def clear(side=side):
            for v in range(2):
                row = 0 if side == 0 else planes + 1
                g_ref[v, row] = jnp.zeros(g_ref.shape[2:], g_ref.dtype)
        when(s == (0 if side == 0 else S - 1), clear)

    for k in range(1, Z):
        for u in range(units):
            for side in range(2):
                zz = z - k if side == 0 else z + k
                have = zz >= 0 if side == 0 else zz < Z
                slot = zz * Y + y
                landed(have, u, slot)
                if k < Z - 1:
                    along(have, u, slot, block(u, slot), side)
                across(have, u, slot, block(u, slot))
                rim(have, u, slot)
        if k == 1:
            for j in range(1, S // 2):
                slot = lax.rem(s + 2 * j, S)
                arrive(None, wf_ref.at[slot], wrecv.at[slot])
                send(None, wf_ref.at[slot], wf_ref.at[slot], wsend.at[S // 2 + j], wrecv.at[slot], (mate, c))
    for direct in range(2):
        for k in range(n // 2):
            slot = 2 * k + core
            have = x == k % pair if direct == 0 else x != k % pair
            piece = wg_ref.at[slot]
            arrive(have, piece, precv.at[slot])
            if direct == 0:
                for j in range(1, pair):
                    send(have, piece, piece, xsend.at[j, k], precv.at[slot], (lax.rem(s + 2 * j, S), c))
            send(have, piece, piece, fsend.at[k], precv.at[slot], (mate, c))
    for k in range(Z):
        for u in range(units):
            for peer in ypeer:
                for side in range(2 if k else 1):
                    zz = z - k if side == 0 else z + k
                    have = None if k == 0 else zz >= 0 if side == 0 else zz < Z
                    slot = zz * Y + peer - z * Y
                    landed(have, u, slot)
                    rim(have, u, slot)
    for u in range(units):
        pltpu.make_async_copy(own(u), block(u, c), lsem.at[u]).wait()
    pltpu.make_async_copy(w_ref, wf_ref.at[s], lsem.at[units]).wait()
    for j in range(S // 2):
        slot = lax.rem(mate + 2 * j, S)
        arrive(None, wf_ref.at[slot], wrecv.at[slot])
    for k in range(n // 2):
        slot = 2 * k + 1 - core
        arrive(None, wg_ref.at[slot], precv.at[slot])
    for v in range(2):
        for slot in range(n):
            arrive(s > 0, g_ref.at[v, 0, slot], hrecv.at[v, 0, slot])
            arrive(s < S - 1, g_ref.at[v, planes + 1, slot], hrecv.at[v, 1, slot])
    for cond, make in sent:
        when(cond, lambda make=make: make().wait_send())


def conv_kernel(g_ref, wf_ref, wg_ref, o_ref, k_ref):
    S, _, lc, width = wf_ref.shape
    n = wg_ref.shape[0]
    planes = o_ref.shape[1]
    cells = o_ref.shape[3]
    pack = LANES // lc
    for t in range(TAPS):
        rows = pl.ds(t * lc, lc)
        k_ref[0, rows, :] = jnp.concatenate([wf_ref[i, t] for i in range(S)], axis=-1)
        f = TAPS - 1 - t
        at = (f % pack) * lc
        k_ref[1, rows, :] = jnp.concatenate([wg_ref[i, f // pack][:, at:at + lc] for i in range(n)], axis=-1)
    lane = lax.broadcasted_iota(jnp.int32, (lc, cells), 1)
    row, col = lane // COLS, lane % COLS
    nine = 9 * lc

    def step(k, carry):
        v, d = k // planes, k % planes
        total = None
        for a in range(3):
            part = jnp.dot(k_ref[v, pl.ds(a * nine, nine), :], g_ref[v, d + a], preferred_element_type=jnp.float32)
            total = part if total is None else total + part
        result = None
        for b in range(3):
            lines = None
            for c in range(3):
                at = (3 * b + c) * lc
                piece = total[at:at + lc]
                if c != 1:
                    piece = pltpu.roll(piece, (1 - c) % cells, 1)
                    piece = jnp.where(col == (0 if c == 0 else COLS - 1), 0.0, piece)
                lines = piece if lines is None else lines + piece
            if b != 1:
                lines = pltpu.roll(lines, ((1 - b) * COLS) % cells, 1)
                lines = jnp.where(row == (0 if b == 0 else ROWS - 1), 0.0, lines)
            result = lines if result is None else result + lines
        o_ref[v, d] = result.astype(o_ref.dtype)
        return carry

    lax.fori_loop(0, 2 * planes, step, 0)


def general(S, n, inputs, weights, cotangent):
    lc, planes, cells = inputs.shape
    wide = weights.shape[2]
    r = wide // lc
    C = n * lc
    Y = max(d for d in range(1, n + 1) if n % d == 0 and 2 * d * d <= n)
    Z = n // Y
    volumes = jnp.stack((inputs, cotangent)).transpose(0, 2, 1, 3)
    pack = LANES // lc
    nt = -(-TAPS // pack)
    padded = jnp.pad(weights, ((0, nt * pack - TAPS), (0, 0), (0, 0)))
    pieces = padded.reshape(nt, pack, lc, r, lc).transpose(3, 0, 4, 1, 2).reshape(r, nt, lc, pack * lc)
    vmem = pl.BlockSpec(memory_space=pltpu.VMEM)
    anyspace = pl.BlockSpec(memory_space=pl.ANY)
    dma = pltpu.SemaphoreType.DMA
    bf16 = jnp.bfloat16
    gathered, wf, wg = pl.pallas_call(
        functools.partial(gather_kernel, S, Z, Y, r),
        out_shape=(jax.ShapeDtypeStruct((2, planes + 2, n, lc, cells), bf16),
                   jax.ShapeDtypeStruct((S,) + weights.shape, bf16),
                   jax.ShapeDtypeStruct((n,) + pieces.shape[1:], bf16)),
        in_specs=[anyspace] * 3,
        out_specs=(vmem,) * 3,
        scratch_shapes=[dma((2 * H + 1,)), dma((2 * H, 2, n)), dma((2 * H, Y - 1, n)), dma((2 * H, n)), dma((2, 2, n)), dma((2, 2, n)),
                        dma((S,)), dma((S,)), dma((r,)), dma((n // 2,)), dma((S // 2, n // 2)), dma((n,))],
        compiler_params=pltpu.CompilerParams(collective_id=0, has_side_effects=True, vmem_limit_bytes=40 << 20),
        name="gather",
    )(volumes, weights, pieces)
    out = pl.pallas_call(
        conv_kernel,
        out_shape=jax.ShapeDtypeStruct((2, planes, lc, cells), bf16),
        in_specs=[vmem] * 3,
        out_specs=vmem,
        scratch_shapes=[pltpu.VMEM((2, TAPS * lc, C), bf16)],
        compiler_params=pltpu.CompilerParams(vmem_limit_bytes=48 << 20),
        name="conv",
    )(gathered.reshape(2, planes + 2, C, cells), wf, wg)
    out = out.transpose(0, 2, 1, 3)
    return out[0], out[1]


def ranges(planes):
    return [(planes - 1, 1)] + [(p, 2) for p in range(0, planes - 2, 2)] + [(planes - 2, 1)]


def split_kernel(x_ref, w_ref, out_ref, g_ref, wst_ref, stage_ref, k_ref, ob_ref,
                 asend, arecv, ysend, hsend, hrecv, wsend, wrecv, srecv, osend, orecv):
    planes, n = ob_ref.shape[0], g_ref.shape[1]
    lc, cells = g_ref.shape[2:]
    C = n * lc
    chunks = ranges(planes)
    s, c = lax.axis_index("slab"), lax.axis_index("chan")
    z, y = lax.div(c, 2), lax.rem(c, 2)
    x, core = lax.div(s, 2), lax.rem(s, 2)
    h = lax.div(z, 2)
    part = TAPS // PIECES
    outer = lax.rem(z, 3) == 0
    inner = jnp.logical_not(outer)
    odd = lax.rem(z + y, 2) == 1
    b = z - 2 * h
    zp = 4 * h + 1 - z
    v = jnp.where(outer, 0, 1)
    mate, xpeer = s + 1 - 2 * core, s + 2 - 4 * x
    ypeer = 2 * z + 1 - y
    MESH = pl.DeviceIdType.MESH

    ring = [lax.rem(z + j, 4) for j in range(1, 4)]
    near, same = x == h, core == y
    other = jnp.logical_not(same)
    home_w = jnp.logical_and(inner, near)
    cross_w = jnp.logical_and(inner, jnp.logical_not(near))
    swap = (mate, ypeer)
    diag = (3 - s, ypeer)

    links = [(None, (mate, c)), (None, (xpeer, c)), (None, (s, ypeer))]
    links += [(None, (s, 2 * zz + y)) for zz in ring]
    links += [(x != core, (3 - s, c)), (odd, (s, 2 * zp + 1 - y))]
    links += [(jnp.logical_and(other, jnp.logical_or(outer, near)), swap), (jnp.logical_and(other, inner), diag)]
    barrier = pltpu.get_barrier_semaphore()
    for cond, peer in links:
        when(cond, functools.partial(pl.semaphore_signal, barrier, inc=1, device_id=peer, device_id_type=MESH))
    pl.semaphore_wait(barrier, sum(1 if cond is None else cond.astype(jnp.int32) for cond, _ in links))

    sent = []

    def send(cond, src, dst, ssem, rsem, to):
        def make():
            return pltpu.make_async_remote_copy(src_ref=src, dst_ref=dst, send_sem=ssem, recv_sem=rsem,
                                                device_id=to, device_id_type=MESH)
        when(cond, lambda: make().start())
        sent.append((cond, make))

    def local(cond, src, dst, sem):
        when(cond, lambda: pltpu.make_async_copy(src, dst, sem).start())

    def arrive(cond, dst, sem):
        when(cond, lambda: pltpu.make_async_copy(dst, dst, sem).wait())

    def piece(ref, i):
        return ref.at[pl.ds(i * part, part)]

    def shard(p, q, i):
        return wst_ref.at[p, pl.ds(i * part, part), pl.ds(pl.multiple_of(q * lc, lc), lc)]

    def block(i, slot):
        return g_ref.at[pl.ds(1 + chunks[i][0], chunks[i][1]), slot]

    def own(u, i):
        return x_ref.at[u, pl.ds(*chunks[i])]

    through = (s, 2 * jnp.where(outer, 1 + x, 3 - z) + y)
    for i in range(PIECES):
        mine = piece(w_ref, i)
        for m, (cond, dst, sem, to) in enumerate((
                (jnp.logical_and(outer, same), shard(z, core, i), wrecv.at[z, core, i], through),
                (jnp.logical_and(outer, other), piece(stage_ref, i), srecv.at[i], swap),
                (jnp.logical_and(home_w, other), shard(z, 1 - core, i), wrecv.at[z, 1 - core, i], swap),
                (jnp.logical_and(cross_w, same), piece(stage_ref, i), srecv.at[i], (xpeer, c)),
                (jnp.logical_and(cross_w, other), piece(stage_ref, i), srecv.at[i], diag))):
            send(cond, mine, dst, wsend.at[0], sem, to)
        local(jnp.logical_and(home_w, same), mine, shard(z, core, i), wrecv.at[z, core, i])
        local(outer, mine, shard(s, b, i), wrecv.at[s, b, i])
    for i in range(PIECES):
        mine = piece(w_ref, i)
        send(inner, mine, shard(s, b, i), wsend.at[1], wrecv.at[s, b, i], (s, 2 * zp + y))
        send(outer, mine, shard(s, b, i), wsend.at[2], wrecv.at[s, b, i], (xpeer, c))
        send(outer, mine, shard(s, b, i), wsend.at[3], wrecv.at[s, b, i], (mate, c))

    def depart(i):
        for zz in ring:
            send(None, own(jnp.where(lax.rem(zz, 3) == 0, 0, 1), i), block(i, c), asend.at[zz], arecv.at[i, c],
                 (s, 2 * zz + y))
        send(None, own(v, i), block(i, c), ysend.at[z], arecv.at[i, c], (s, ypeer))
        local(None, own(v, i), block(i, c), arecv.at[i, c])

    def clear():
        for edge in range(2):
            def zero(edge=edge):
                row = 0 if edge == 0 else planes + 1
                g_ref[row] = jnp.zeros(g_ref.shape[1:], g_ref.dtype)
            when(s == (0 if edge == 0 else 3), zero)

    def rim(i, slot):
        first, count = chunks[i]
        if first + count == planes:
            send(s < 3, g_ref.at[planes, slot], g_ref.at[0, slot], hsend.at[0], hrecv.at[0], (s + 1, c))
        if first == 0:
            send(s > 0, g_ref.at[1, slot], g_ref.at[planes + 1, slot], hsend.at[1], hrecv.at[1],
                 (s - 1, c))

    def column(i):
        for j, zz in enumerate([z, *ring]):
            slot = 2 * zz + y
            arrive(None, block(i, slot), arecv.at[i, slot])
            if j:
                send(None, block(i, slot), block(i, slot), ysend.at[zz], arecv.at[i, slot], (s, ypeer))
            rim(i, slot)

    def across(i):
        for zz in [z, *ring]:
            slot = 2 * zz + 1 - y
            arrive(None, block(i, slot), arecv.at[i, slot])
            rim(i, slot)

    def order(near_z, far_z, out):
        return jnp.where(outer, out, jnp.where(near, near_z, far_z))

    pairs = [order(z, z, s), order(3 * h, 3 - z, mate), order(3 - 3 * h, 3 * h, xpeer), order(3 - z, 3 - 3 * h, 3 - s)]
    first = [(jnp.where(outer, s if j < 2 else xpeer, pairs[j]), jnp.where(outer, b if j % 2 == 0 else 1 - b, core))
             for j in range(4)]
    second = [(jnp.where(outer, mate if j < 2 else 3 - s, pairs[j]),
               jnp.where(outer, b if j % 2 == 0 else 1 - b, 1 - core)) for j in range(4)]

    def weights(j, pieces=range(PIECES), cond=None):
        p, q = first[j]
        for i in pieces:
            ref, sem = shard(p, q, i), wrecv.at[p, q, i]
            arrive(cond, ref, sem)
            if j < 3:
                send(both(cond, None if j == 1 else home_w), ref, ref, wsend.at[5 + j], sem, (xpeer, c))
            send(both(cond, None if j else inner), ref, ref, wsend.at[8 + j], sem, (mate, c))

    def fetched(j):
        p, q = second[j]
        for i in range(PIECES):
            arrive(None, shard(p, q, i), wrecv.at[p, q, i])

    def forward(i):
        relay = jnp.where(outer, other, near)
        arrive(relay, piece(stage_ref, i), srecv.at[i])
        send(relay, piece(stage_ref, i), shard(z, core, i), wsend.at[4], wrecv.at[z, core, i], through)

    def build(*ks):
        def tap(t, carry):
            p = pairs[ks[0]] if len(ks) == 1 else jnp.where(t < TAPS, pairs[ks[0]], pairs[ks[1]])
            t = lax.rem(t, TAPS)
            rows = pl.ds(pl.multiple_of(lax.rem(t, 9) * 2 * lc, 2 * lc), 2 * lc)
            cols = pl.ds(pl.multiple_of(lax.div(t, 9) * C + p * 2 * lc, 2 * lc), 2 * lc)

            def plain():
                k_ref[rows, cols] = wst_ref[p, t]

            def turned():
                k_ref[rows, cols] = wst_ref[p, TAPS - 1 - t].T
            pl.when(outer)(plain)
            pl.when(inner)(turned)
            return carry
        lax.fori_loop(0, TAPS * len(ks), tap, 0)

    def finish(k):
        p, (m, q) = pairs[k], second[k]

        def tap(t, carry):
            at = jnp.where(outer, t, TAPS - 1 - t)
            rows = pl.ds(pl.multiple_of(lax.rem(at, 9) * 2 * lc, 2 * lc), 2 * lc)
            cols = pl.ds(pl.multiple_of(lax.div(at, 9) * C + p * 2 * lc, 2 * lc), 2 * lc)

            def plain():
                k_ref[rows, cols] = wst_ref[p, t]

            def turned():
                k_ref[rows, cols] = wst_ref[p, t].T
            pl.when(outer)(plain)
            pl.when(inner)(turned)
            return carry

        def step(i, carry):
            arrive(None, shard(m, q, i), wrecv.at[m, q, i])
            return lax.fori_loop(i * part, (i + 1) * part, tap, carry)
        lax.fori_loop(0, PIECES, step, 0)

    lane = lax.broadcasted_iota(jnp.int32, (2 * lc, cells), 1)
    row, col = lane // COLS, lane % COLS

    def product(d):
        rhs = g_ref[pl.ds(d, 3)].reshape(3 * C, cells)
        return jnp.dot(k_ref[...], rhs, preferred_element_type=jnp.float32)

    def gathered(total):
        result = None
        for t in range(3):
            lines = None
            for u in range(3):
                at = (3 * t + u) * 2 * lc
                piece = total[at:at + 2 * lc]
                if u != 1:
                    piece = pltpu.roll(piece, (1 - u) % cells, 1)
                    piece = jnp.where(col == (0 if u == 0 else COLS - 1), 0.0, piece)
                lines = piece if lines is None else lines + piece
            if t != 1:
                lines = pltpu.roll(lines, ((1 - t) * COLS) % cells, 1)
                lines = jnp.where(row == (0 if t == 0 else ROWS - 1), 0.0, lines)
            result = lines if result is None else result + lines
        return result

    home = z == 2 * h + y

    def parcel(d, q):
        stay = jnp.where(outer, b == q, jnp.logical_and(home, y == q))
        to = (s, jnp.where(outer, 2 * (2 * h + q) + y, 2 * (2 * h + y) + q))
        return stay, pltpu.make_async_remote_copy(
            src_ref=ob_ref.at[d, q], dst_ref=out_ref.at[v, d], send_sem=osend.at[q], recv_sem=orecv.at[v],
            device_id=to, device_id_type=MESH)

    def deliver(d, result):
        ob_ref[d] = result.reshape(2, lc, cells).astype(ob_ref.dtype)
        for q in range(2):
            stay, copy = parcel(d, q)
            when(jnp.logical_not(stay), copy.start)
            local(stay, ob_ref.at[d, q], out_ref.at[v, d], orecv.at[v])

    def run():
        def one(d, carry):
            arrive(jnp.logical_and(d == 0, s > 0), g_ref.at[0], hrecv.at[0])
            arrive(jnp.logical_and(d == planes - 1, s < 3), g_ref.at[planes + 1], hrecv.at[1])
            for i in range(3, len(chunks)):
                if i > 3:
                    pl.when(d == 1)(functools.partial(column, i))
                pl.when(d == chunks[i][0] - 1)(functools.partial(across, i))
            deliver(d, gathered(product(d)))
            return carry
        lax.fori_loop(0, planes, one, 0)

    depart(0)
    depart(1)
    clear()
    weights(0)
    forward(0)
    weights(1, [0])
    forward(1)
    weights(1, [1])
    forward(2)
    weights(1, [2])
    depart(2)
    weights(2, cond=home_w)
    column(0)
    column(1)
    depart(3)
    fetched(0)
    fetched(1)
    build(0, 1)
    weights(2, cond=jnp.logical_not(home_w))
    across(0)
    across(1)
    column(2)
    depart(4)
    fetched(2)
    weights(3)
    build(2)
    across(2)
    column(3)
    finish(3)
    run()
    for u in range(2):
        arrive(None, out_ref.at[u], orecv.at[u])
        stay, _ = parcel(0, u)
        arrive(jnp.logical_not(stay), ob_ref.at[:, u], osend.at[u])
    for zz in ring:
        arrive(None, g_ref.at[pl.ds(1, planes), 0], asend.at[zz])
    for zz in range(4):
        arrive(None, g_ref.at[pl.ds(1, planes), 0], ysend.at[zz])
    arrive(s < 3, g_ref.at[0], hsend.at[0])
    arrive(s > 0, g_ref.at[0], hsend.at[1])
    kinds = [jnp.logical_not(jnp.logical_and(home_w, same)), inner, outer, outer,
             jnp.where(outer, other, near), home_w, None, home_w, inner, None, None, None]
    for m, cond in enumerate(kinds):
        arrive(cond, stage_ref, wsend.at[m])


def split(n, inputs, weights, cotangent):
    lc, planes, cells = inputs.shape
    volumes = jnp.stack((inputs, cotangent)).transpose(0, 2, 1, 3)
    dma = pltpu.SemaphoreType.DMA
    bf16 = jnp.bfloat16
    count = len(ranges(planes))
    out = pl.pallas_call(
        split_kernel,
        out_shape=jax.ShapeDtypeStruct((2, planes, lc, cells), bf16),
        in_specs=[pl.BlockSpec(memory_space=pl.ANY), pl.BlockSpec(memory_space=pltpu.HBM)],
        out_specs=pl.BlockSpec(memory_space=pltpu.VMEM),
        scratch_shapes=[pltpu.VMEM((planes + 2, n, lc, cells), bf16),
                        pltpu.VMEM((n // 2, TAPS, 2 * lc, weights.shape[2]), bf16),
                        pltpu.VMEM(weights.shape, bf16),
                        pltpu.VMEM((9 * 2 * lc, 3 * n * lc), bf16),
                        pltpu.VMEM((planes, 2, lc, cells), bf16),
                        dma((4,)), dma((count, n)), dma((4,)), dma((2,)), dma((2,)),
                        dma((12,)), dma((n // 2, 2, PIECES)), dma((PIECES,)), dma((2,)), dma((2,))],
        compiler_params=pltpu.CompilerParams(collective_id=1, has_side_effects=True, vmem_limit_bytes=48 << 20),
        name="split",
    )(volumes, weights)
    out = out.transpose(0, 2, 1, 3)
    return out[0], out[1]


def body(S, n, inputs, weights, cotangent):
    lc = inputs.shape[0]
    if (S, n) == (4, 8) and weights.shape[2] == 2 * lc == LANES and inputs.shape[1] == 8:
        return split(n, inputs, weights, cotangent)
    return general(S, n, inputs, weights, cotangent)


def solution(mesh):
    S, n = mesh.shape["slab"], mesh.shape["chan"]
    return jax.shard_map(
        functools.partial(body, S, n),
        mesh=mesh,
        in_specs=(P("chan", "slab", None), P(None, "chan", "slab"), P("chan", "slab", None)),
        out_specs=(P("chan", "slab", None), P("chan", "slab", None)),
        check_vma=False,
    )
```

```python
import functools

import jax
import jax.numpy as jnp
from jax import lax
from jax.experimental import pallas as pl
from jax.experimental.pallas import tpu as pltpu
from jax.sharding import PartitionSpec as P

ROWS = 8
COLS = 32
TAPS = 27
LANES = 128
H = 2
PIECES = 3


def when(cond, fn):
    if cond is None:
        fn()
    else:
        pl.when(cond)(fn)


def both(a, b):
    return b if a is None else a if b is None else jnp.logical_and(a, b)


def gather_kernel(S, Z, Y, r, x_ref, w_ref, p_ref, g_ref, wf_ref, wg_ref,
                  lsem, vsend, ysend, vrecv, hsend, hrecv, wsend, wrecv, psend, fsend, xsend, precv):
    n = Z * Y
    planes = x_ref.shape[1]
    units, part = 2 * H, planes // H
    s, c = lax.axis_index("slab"), lax.axis_index("chan")
    z, y = lax.div(c, Y), lax.rem(c, Y)
    core = lax.rem(s, 2)
    mate = s + 1 - 2 * core
    ypeer = [z * Y + lax.rem(y + j, Y) for j in range(1, Y)]
    up, down = z < Z - 1, z > 0

    barrier = pltpu.get_barrier_semaphore()
    links = [(up, (s, c + Y)), (down, (s, c - Y))]
    links += [(None, (s, peer)) for peer in ypeer]
    links += [(None, (lax.rem(s + j, S), c)) for j in range(1, S)]
    targets = []
    pair = S // 2
    x = lax.div(s, 2)
    host = 2 * lax.rem(lax.div(c, 2), pair) + lax.rem(c, 2)
    for j in range(r):
        to = (host, s * r + j)
        targets.append((jnp.logical_or(to[0] != s, to[1] != c), to, j, j))
    sources = []
    for k in range(n // 2):
        frm = (lax.div(c, r), 2 * k + core)
        other = jnp.logical_or(frm[0] != s, frm[1] != c)
        sources.append((jnp.logical_and(other, x == k % pair), frm))
    links += [(t[0], t[1]) for t in targets] + sources
    for cond, peer in links:
        when(cond, functools.partial(pl.semaphore_signal, barrier, inc=1, device_id=peer,
                                     device_id_type=pl.DeviceIdType.MESH))
    peers = sum(1 if cond is None else cond.astype(jnp.int32) for cond, _ in links)
    pl.semaphore_wait(barrier, peers)

    sent = []

    def send(cond, src, dst, ssem, rsem, to):
        def make():
            return pltpu.make_async_remote_copy(src_ref=src, dst_ref=dst, send_sem=ssem, recv_sem=rsem,
                                                device_id=to, device_id_type=pl.DeviceIdType.MESH)
        when(cond, lambda: make().start())
        sent.append((cond, make))

    def arrive(cond, dst, sem):
        when(cond, lambda: pltpu.make_async_copy(dst, dst, sem).wait())

    def own(u):
        return x_ref.at[u // H, pl.ds(u % H * part, part)]

    def block(u, slot):
        return g_ref.at[u // H, pl.ds(1 + u % H * part, part), slot]

    def along(cond, u, slot, src, side):
        ok, to = (up, (s, c + Y)) if side == 0 else (down, (s, c - Y))
        send(both(cond, ok), src, block(u, slot), vsend.at[u, side, slot], vrecv.at[u, slot], to)

    def across(cond, u, slot, src):
        for j, peer in enumerate(ypeer):
            send(cond, src, block(u, slot), ysend.at[u, j, slot], vrecv.at[u, slot], (s, peer))

    def landed(cond, u, slot):
        arrive(cond, block(u, slot), vrecv.at[u, slot])

    def rim(cond, u, slot, first=None, last=None):
        v = u // H
        if u % H == H - 1:
            last = g_ref.at[v, planes, slot] if last is None else last
            send(both(cond, s < S - 1), last, g_ref.at[v, 0, slot], hsend.at[v, 0, slot], hrecv.at[v, 0, slot],
                 (s + 1, c))
        if u % H == 0:
            first = g_ref.at[v, 1, slot] if first is None else first
            send(both(cond, s > 0), first, g_ref.at[v, planes + 1, slot], hsend.at[v, 1, slot], hrecv.at[v, 1, slot],
                 (s - 1, c))

    for u in range(units):
        for side in range(2):
            along(None, u, c, own(u), side)
        across(None, u, c, own(u))
        if u == H - 1:
            for cond, to, j, k in targets:
                send(cond, p_ref.at[j], wg_ref.at[c], psend.at[k], precv.at[c], to)
    for j in range(1, S // 2):
        send(None, w_ref, wf_ref.at[s], wsend.at[j], wrecv.at[s], (lax.rem(s + 2 * j, S), c))
    send(None, w_ref, wf_ref.at[s], wsend.at[0], wrecv.at[s], (mate, c))
    for u in range(units):
        pltpu.make_async_copy(own(u), block(u, c), lsem.at[u]).start()
        rim(None, u, c, x_ref.at[u // H, 0], x_ref.at[u // H, planes - 1])
    pltpu.make_async_copy(w_ref, wf_ref.at[s], lsem.at[units]).start()
    home = jnp.logical_and(s == lax.div(c, r), s == host)
    when(home, lambda: pltpu.make_async_copy(p_ref.at[lax.rem(c, r)], wg_ref.at[c], precv.at[c]).start())

    for side in range(2):
        def clear(side=side):
            for v in range(2):
                row = 0 if side == 0 else planes + 1
                g_ref[v, row] = jnp.zeros(g_ref.shape[2:], g_ref.dtype)
        when(s == (0 if side == 0 else S - 1), clear)

    for k in range(1, Z):
        for u in range(units):
            for side in range(2):
                zz = z - k if side == 0 else z + k
                have = zz >= 0 if side == 0 else zz < Z
                slot = zz * Y + y
                landed(have, u, slot)
                if k < Z - 1:
                    along(have, u, slot, block(u, slot), side)
                across(have, u, slot, block(u, slot))
                rim(have, u, slot)
        if k == 1:
            for j in range(1, S // 2):
                slot = lax.rem(s + 2 * j, S)
                arrive(None, wf_ref.at[slot], wrecv.at[slot])
                send(None, wf_ref.at[slot], wf_ref.at[slot], wsend.at[S // 2 + j], wrecv.at[slot], (mate, c))
    for direct in range(2):
        for k in range(n // 2):
            slot = 2 * k + core
            have = x == k % pair if direct == 0 else x != k % pair
            piece = wg_ref.at[slot]
            arrive(have, piece, precv.at[slot])
            if direct == 0:
                for j in range(1, pair):
                    send(have, piece, piece, xsend.at[j, k], precv.at[slot], (lax.rem(s + 2 * j, S), c))
            send(have, piece, piece, fsend.at[k], precv.at[slot], (mate, c))
    for k in range(Z):
        for u in range(units):
            for peer in ypeer:
                for side in range(2 if k else 1):
                    zz = z - k if side == 0 else z + k
                    have = None if k == 0 else zz >= 0 if side == 0 else zz < Z
                    slot = zz * Y + peer - z * Y
                    landed(have, u, slot)
                    rim(have, u, slot)
    for u in range(units):
        pltpu.make_async_copy(own(u), block(u, c), lsem.at[u]).wait()
    pltpu.make_async_copy(w_ref, wf_ref.at[s], lsem.at[units]).wait()
    for j in range(S // 2):
        slot = lax.rem(mate + 2 * j, S)
        arrive(None, wf_ref.at[slot], wrecv.at[slot])
    for k in range(n // 2):
        slot = 2 * k + 1 - core
        arrive(None, wg_ref.at[slot], precv.at[slot])
    for v in range(2):
        for slot in range(n):
            arrive(s > 0, g_ref.at[v, 0, slot], hrecv.at[v, 0, slot])
            arrive(s < S - 1, g_ref.at[v, planes + 1, slot], hrecv.at[v, 1, slot])
    for cond, make in sent:
        when(cond, lambda make=make: make().wait_send())


def conv_kernel(g_ref, wf_ref, wg_ref, o_ref, k_ref):
    S, _, lc, width = wf_ref.shape
    n = wg_ref.shape[0]
    planes = o_ref.shape[1]
    cells = o_ref.shape[3]
    pack = LANES // lc
    for t in range(TAPS):
        rows = pl.ds(t * lc, lc)
        k_ref[0, rows, :] = jnp.concatenate([wf_ref[i, t] for i in range(S)], axis=-1)
        f = TAPS - 1 - t
        at = (f % pack) * lc
        k_ref[1, rows, :] = jnp.concatenate([wg_ref[i, f // pack][:, at:at + lc] for i in range(n)], axis=-1)
    lane = lax.broadcasted_iota(jnp.int32, (lc, cells), 1)
    row, col = lane // COLS, lane % COLS
    nine = 9 * lc

    def step(k, carry):
        v, d = k // planes, k % planes
        total = None
        for a in range(3):
            part = jnp.dot(k_ref[v, pl.ds(a * nine, nine), :], g_ref[v, d + a], preferred_element_type=jnp.float32)
            total = part if total is None else total + part
        result = None
        for b in range(3):
            lines = None
            for c in range(3):
                at = (3 * b + c) * lc
                piece = total[at:at + lc]
                if c != 1:
                    piece = pltpu.roll(piece, (1 - c) % cells, 1)
                    piece = jnp.where(col == (0 if c == 0 else COLS - 1), 0.0, piece)
                lines = piece if lines is None else lines + piece
            if b != 1:
                lines = pltpu.roll(lines, ((1 - b) * COLS) % cells, 1)
                lines = jnp.where(row == (0 if b == 0 else ROWS - 1), 0.0, lines)
            result = lines if result is None else result + lines
        o_ref[v, d] = result.astype(o_ref.dtype)
        return carry

    lax.fori_loop(0, 2 * planes, step, 0)


def general(S, n, inputs, weights, cotangent):
    lc, planes, cells = inputs.shape
    wide = weights.shape[2]
    r = wide // lc
    C = n * lc
    Y = max(d for d in range(1, n + 1) if n % d == 0 and 2 * d * d <= n)
    Z = n // Y
    volumes = jnp.stack((inputs, cotangent)).transpose(0, 2, 1, 3)
    pack = LANES // lc
    nt = -(-TAPS // pack)
    padded = jnp.pad(weights, ((0, nt * pack - TAPS), (0, 0), (0, 0)))
    pieces = padded.reshape(nt, pack, lc, r, lc).transpose(3, 0, 4, 1, 2).reshape(r, nt, lc, pack * lc)
    vmem = pl.BlockSpec(memory_space=pltpu.VMEM)
    anyspace = pl.BlockSpec(memory_space=pl.ANY)
    dma = pltpu.SemaphoreType.DMA
    bf16 = jnp.bfloat16
    gathered, wf, wg = pl.pallas_call(
        functools.partial(gather_kernel, S, Z, Y, r),
        out_shape=(jax.ShapeDtypeStruct((2, planes + 2, n, lc, cells), bf16),
                   jax.ShapeDtypeStruct((S,) + weights.shape, bf16),
                   jax.ShapeDtypeStruct((n,) + pieces.shape[1:], bf16)),
        in_specs=[anyspace] * 3,
        out_specs=(vmem,) * 3,
        scratch_shapes=[dma((2 * H + 1,)), dma((2 * H, 2, n)), dma((2 * H, Y - 1, n)), dma((2 * H, n)), dma((2, 2, n)), dma((2, 2, n)),
                        dma((S,)), dma((S,)), dma((r,)), dma((n // 2,)), dma((S // 2, n // 2)), dma((n,))],
        compiler_params=pltpu.CompilerParams(collective_id=0, has_side_effects=True, vmem_limit_bytes=40 << 20),
        name="gather",
    )(volumes, weights, pieces)
    out = pl.pallas_call(
        conv_kernel,
        out_shape=jax.ShapeDtypeStruct((2, planes, lc, cells), bf16),
        in_specs=[vmem] * 3,
        out_specs=vmem,
        scratch_shapes=[pltpu.VMEM((2, TAPS * lc, C), bf16)],
        compiler_params=pltpu.CompilerParams(vmem_limit_bytes=48 << 20),
        name="conv",
    )(gathered.reshape(2, planes + 2, C, cells), wf, wg)
    out = out.transpose(0, 2, 1, 3)
    return out[0], out[1]


def ranges(planes):
    return [(planes - 1, 1)] + [(p, 2) for p in range(0, planes - 2, 2)] + [(planes - 2, 1)]


def split_kernel(x_ref, w_ref, out_ref, g_ref, wst_ref, stage_ref, k_ref, ob_ref,
                 asend, arecv, ysend, hsend, hrecv, wsend, wrecv, srecv, osend, orecv):
    planes, n = ob_ref.shape[0], g_ref.shape[1]
    lc, cells = g_ref.shape[2:]
    C = n * lc
    chunks = ranges(planes)
    s, c = lax.axis_index("slab"), lax.axis_index("chan")
    z, y = lax.div(c, 2), lax.rem(c, 2)
    x, core = lax.div(s, 2), lax.rem(s, 2)
    h = lax.div(z, 2)
    part = TAPS // PIECES
    outer = lax.rem(z, 3) == 0
    inner = jnp.logical_not(outer)
    odd = lax.rem(z + y, 2) == 1
    b = z - 2 * h
    zp = 4 * h + 1 - z
    v = jnp.where(outer, 0, 1)
    mate, xpeer = s + 1 - 2 * core, s + 2 - 4 * x
    ypeer = 2 * z + 1 - y
    MESH = pl.DeviceIdType.MESH

    ring = [zp, 2 - h, 3 - 3 * h]
    near, same = x == h, core == y
    other = jnp.logical_not(same)
    home_w = jnp.logical_and(inner, near)
    cross_w = jnp.logical_and(inner, jnp.logical_not(near))
    swap = (mate, ypeer)
    diag = (3 - s, ypeer)

    links = [(None, (mate, c)), (None, (xpeer, c)), (None, (s, ypeer))]
    links += [(None, (s, 2 * zz + y)) for zz in ring]
    links += [(x != core, (3 - s, c)), (odd, (s, 2 * zp + 1 - y))]
    links += [(jnp.logical_and(other, jnp.logical_or(outer, near)), swap), (jnp.logical_and(other, inner), diag)]
    barrier = pltpu.get_barrier_semaphore()
    for cond, peer in links:
        when(cond, functools.partial(pl.semaphore_signal, barrier, inc=1, device_id=peer, device_id_type=MESH))
    pl.semaphore_wait(barrier, sum(1 if cond is None else cond.astype(jnp.int32) for cond, _ in links))

    sent = []

    def send(cond, src, dst, ssem, rsem, to):
        def make():
            return pltpu.make_async_remote_copy(src_ref=src, dst_ref=dst, send_sem=ssem, recv_sem=rsem,
                                                device_id=to, device_id_type=MESH)
        when(cond, lambda: make().start())
        sent.append((cond, make))

    def local(cond, src, dst, sem):
        when(cond, lambda: pltpu.make_async_copy(src, dst, sem).start())

    def arrive(cond, dst, sem):
        when(cond, lambda: pltpu.make_async_copy(dst, dst, sem).wait())

    def piece(ref, i):
        return ref.at[pl.ds(i * part, part)]

    def shard(p, q, i):
        return wst_ref.at[p, pl.ds(i * part, part), pl.ds(pl.multiple_of(q * lc, lc), lc)]

    def block(i, slot):
        return g_ref.at[pl.ds(1 + chunks[i][0], chunks[i][1]), slot]

    def own(u, i):
        return x_ref.at[u, pl.ds(*chunks[i])]

    through = (s, 2 * jnp.where(outer, 1 + x, 3 - z) + y)
    for i in range(PIECES):
        mine = piece(w_ref, i)
        for m, (cond, dst, sem, to) in enumerate((
                (jnp.logical_and(outer, same), shard(z, core, i), wrecv.at[z, core, i], through),
                (jnp.logical_and(outer, other), piece(stage_ref, i), srecv.at[i], swap),
                (jnp.logical_and(home_w, other), shard(z, 1 - core, i), wrecv.at[z, 1 - core, i], swap),
                (jnp.logical_and(cross_w, same), piece(stage_ref, i), srecv.at[i], (xpeer, c)),
                (jnp.logical_and(cross_w, other), piece(stage_ref, i), srecv.at[i], diag))):
            send(cond, mine, dst, wsend.at[0], sem, to)
        local(jnp.logical_and(home_w, same), mine, shard(z, core, i), wrecv.at[z, core, i])
        local(outer, mine, shard(s, b, i), wrecv.at[s, b, i])
    for i in range(PIECES):
        mine = piece(w_ref, i)
        send(inner, mine, shard(s, b, i), wsend.at[1], wrecv.at[s, b, i], (s, 2 * zp + y))
        send(outer, mine, shard(s, b, i), wsend.at[2], wrecv.at[s, b, i], (xpeer, c))
        send(outer, mine, shard(s, b, i), wsend.at[3], wrecv.at[s, b, i], (mate, c))

    def depart(i):
        for zz in ring:
            send(None, own(jnp.where(lax.rem(zz, 3) == 0, 0, 1), i), block(i, c), asend.at[zz], arecv.at[i, c],
                 (s, 2 * zz + y))
        send(None, own(v, i), block(i, c), ysend.at[z], arecv.at[i, c], (s, ypeer))
        local(None, own(v, i), block(i, c), arecv.at[i, c])

    def clear():
        for edge in range(2):
            def zero(edge=edge):
                row = 0 if edge == 0 else planes + 1
                g_ref[row] = jnp.zeros(g_ref.shape[1:], g_ref.dtype)
            when(s == (0 if edge == 0 else 3), zero)

    def rim(i, slot):
        first, count = chunks[i]
        if first + count == planes:
            send(s < 3, g_ref.at[planes, slot], g_ref.at[0, slot], hsend.at[0], hrecv.at[0], (s + 1, c))
        if first == 0:
            send(s > 0, g_ref.at[1, slot], g_ref.at[planes + 1, slot], hsend.at[1], hrecv.at[1],
                 (s - 1, c))

    def column(i):
        for j, zz in enumerate([z, *ring]):
            slot = 2 * zz + y
            arrive(None, block(i, slot), arecv.at[i, slot])
            if j:
                send(None, block(i, slot), block(i, slot), ysend.at[zz], arecv.at[i, slot], (s, ypeer))
            rim(i, slot)

    def across(i):
        for zz in [z, *ring]:
            slot = 2 * zz + 1 - y
            arrive(None, block(i, slot), arecv.at[i, slot])
            rim(i, slot)

    def order(near_z, far_z, out):
        return jnp.where(outer, out, jnp.where(near, near_z, far_z))

    pairs = [order(z, z, s), order(3 * h, 3 - z, mate), order(3 - 3 * h, 3 * h, xpeer), order(3 - z, 3 - 3 * h, 3 - s)]
    first = [(jnp.where(outer, s if j < 2 else xpeer, pairs[j]), jnp.where(outer, b if j % 2 == 0 else 1 - b, core))
             for j in range(4)]
    second = [(jnp.where(outer, mate if j < 2 else 3 - s, pairs[j]),
               jnp.where(outer, b if j % 2 == 0 else 1 - b, 1 - core)) for j in range(4)]

    def weights(j, pieces=range(PIECES), cond=None):
        p, q = first[j]
        for i in pieces:
            ref, sem = shard(p, q, i), wrecv.at[p, q, i]
            arrive(cond, ref, sem)
            if j < 3:
                send(both(cond, None if j == 1 else home_w), ref, ref, wsend.at[5 + j], sem, (xpeer, c))
            send(both(cond, None if j else inner), ref, ref, wsend.at[8 + j], sem, (mate, c))

    def fetched(j):
        p, q = second[j]
        for i in range(PIECES):
            arrive(None, shard(p, q, i), wrecv.at[p, q, i])

    def forward(i):
        relay = jnp.where(outer, other, near)
        arrive(relay, piece(stage_ref, i), srecv.at[i])
        send(relay, piece(stage_ref, i), shard(z, core, i), wsend.at[4], wrecv.at[z, core, i], through)

    def build(*ks):
        def tap(t, carry):
            p = pairs[ks[0]] if len(ks) == 1 else jnp.where(t < TAPS, pairs[ks[0]], pairs[ks[1]])
            t = lax.rem(t, TAPS)
            rows = pl.ds(pl.multiple_of(lax.rem(t, 9) * 2 * lc, 2 * lc), 2 * lc)
            cols = pl.ds(pl.multiple_of(lax.div(t, 9) * C + p * 2 * lc, 2 * lc), 2 * lc)

            def plain():
                k_ref[rows, cols] = wst_ref[p, t]

            def turned():
                k_ref[rows, cols] = wst_ref[p, TAPS - 1 - t].T
            pl.when(outer)(plain)
            pl.when(inner)(turned)
            return carry
        lax.fori_loop(0, TAPS * len(ks), tap, 0)

    def finish(k):
        p, (m, q) = pairs[k], second[k]

        def tap(t, carry):
            at = jnp.where(outer, t, TAPS - 1 - t)
            rows = pl.ds(pl.multiple_of(lax.rem(at, 9) * 2 * lc, 2 * lc), 2 * lc)
            cols = pl.ds(pl.multiple_of(lax.div(at, 9) * C + p * 2 * lc, 2 * lc), 2 * lc)

            def plain():
                k_ref[rows, cols] = wst_ref[p, t]

            def turned():
                k_ref[rows, cols] = wst_ref[p, t].T
            pl.when(outer)(plain)
            pl.when(inner)(turned)
            return carry

        def step(i, carry):
            arrive(None, shard(m, q, i), wrecv.at[m, q, i])
            return lax.fori_loop(i * part, (i + 1) * part, tap, carry)
        lax.fori_loop(0, PIECES, step, 0)

    lane = lax.broadcasted_iota(jnp.int32, (2 * lc, cells), 1)
    row, col = lane // COLS, lane % COLS

    def product(d):
        rhs = g_ref[pl.ds(d, 3)].reshape(3 * C, cells)
        return jnp.dot(k_ref[...], rhs, preferred_element_type=jnp.float32)

    def gathered(total):
        result = None
        for t in range(3):
            lines = None
            for u in range(3):
                at = (3 * t + u) * 2 * lc
                piece = total[at:at + 2 * lc]
                if u != 1:
                    piece = pltpu.roll(piece, (1 - u) % cells, 1)
                    piece = jnp.where(col == (0 if u == 0 else COLS - 1), 0.0, piece)
                lines = piece if lines is None else lines + piece
            if t != 1:
                lines = pltpu.roll(lines, ((1 - t) * COLS) % cells, 1)
                lines = jnp.where(row == (0 if t == 0 else ROWS - 1), 0.0, lines)
            result = lines if result is None else result + lines
        return result

    home = z == 2 * h + y

    def parcel(d, q):
        stay = jnp.where(outer, b == q, jnp.logical_and(home, y == q))
        to = (s, jnp.where(outer, 2 * (2 * h + q) + y, 2 * (2 * h + y) + q))
        return stay, pltpu.make_async_remote_copy(
            src_ref=ob_ref.at[d, q], dst_ref=out_ref.at[v, d], send_sem=osend.at[q], recv_sem=orecv.at[v],
            device_id=to, device_id_type=MESH)

    def deliver(d, result):
        ob_ref[d] = result.reshape(2, lc, cells).astype(ob_ref.dtype)
        for q in range(2):
            stay, copy = parcel(d, q)
            when(jnp.logical_not(stay), copy.start)
            local(stay, ob_ref.at[d, q], out_ref.at[v, d], orecv.at[v])

    def run():
        def one(d, carry):
            arrive(jnp.logical_and(d == 0, s > 0), g_ref.at[0], hrecv.at[0])
            arrive(jnp.logical_and(d == planes - 1, s < 3), g_ref.at[planes + 1], hrecv.at[1])
            for i in range(3, len(chunks)):
                if i > 3:
                    pl.when(d == 1)(functools.partial(column, i))
                pl.when(d == chunks[i][0] - 1)(functools.partial(across, i))
            deliver(d, gathered(product(d)))
            return carry
        lax.fori_loop(0, planes, one, 0)

    depart(0)
    depart(1)
    clear()
    weights(0)
    forward(0)
    weights(1, [0])
    forward(1)
    weights(1, [1])
    forward(2)
    weights(1, [2])
    depart(2)
    weights(2, cond=home_w)
    column(0)
    column(1)
    depart(3)
    fetched(0)
    fetched(1)
    build(0, 1)
    weights(2, cond=jnp.logical_not(home_w))
    across(0)
    across(1)
    column(2)
    depart(4)
    fetched(2)
    weights(3)
    build(2)
    across(2)
    column(3)
    finish(3)
    run()
    for u in range(2):
        arrive(None, out_ref.at[u], orecv.at[u])
        stay, _ = parcel(0, u)
        arrive(jnp.logical_not(stay), ob_ref.at[:, u], osend.at[u])
    for zz in ring:
        arrive(None, g_ref.at[pl.ds(1, planes), 0], asend.at[zz])
    for zz in range(4):
        arrive(None, g_ref.at[pl.ds(1, planes), 0], ysend.at[zz])
    arrive(s < 3, g_ref.at[0], hsend.at[0])
    arrive(s > 0, g_ref.at[0], hsend.at[1])
    kinds = [jnp.logical_not(jnp.logical_and(home_w, same)), inner, outer, outer,
             jnp.where(outer, other, near), home_w, None, home_w, inner, None, None, None]
    for m, cond in enumerate(kinds):
        arrive(cond, stage_ref, wsend.at[m])


def split(n, inputs, weights, cotangent):
    lc, planes, cells = inputs.shape
    volumes = jnp.stack((inputs, cotangent)).transpose(0, 2, 1, 3)
    dma = pltpu.SemaphoreType.DMA
    bf16 = jnp.bfloat16
    count = len(ranges(planes))
    out = pl.pallas_call(
        split_kernel,
        out_shape=jax.ShapeDtypeStruct((2, planes, lc, cells), bf16),
        in_specs=[pl.BlockSpec(memory_space=pl.ANY), pl.BlockSpec(memory_space=pltpu.HBM)],
        out_specs=pl.BlockSpec(memory_space=pltpu.VMEM),
        scratch_shapes=[pltpu.VMEM((planes + 2, n, lc, cells), bf16),
                        pltpu.VMEM((n // 2, TAPS, 2 * lc, weights.shape[2]), bf16),
                        pltpu.VMEM(weights.shape, bf16),
                        pltpu.VMEM((9 * 2 * lc, 3 * n * lc), bf16),
                        pltpu.VMEM((planes, 2, lc, cells), bf16),
                        dma((4,)), dma((count, n)), dma((4,)), dma((2,)), dma((2,)),
                        dma((12,)), dma((n // 2, 2, PIECES)), dma((PIECES,)), dma((2,)), dma((2,))],
        compiler_params=pltpu.CompilerParams(collective_id=1, has_side_effects=True, vmem_limit_bytes=48 << 20),
        name="split",
    )(volumes, weights)
    out = out.transpose(0, 2, 1, 3)
    return out[0], out[1]


def body(S, n, inputs, weights, cotangent):
    lc = inputs.shape[0]
    if (S, n) == (4, 8) and weights.shape[2] == 2 * lc == LANES and inputs.shape[1] == 8:
        return split(n, inputs, weights, cotangent)
    return general(S, n, inputs, weights, cotangent)


def solution(mesh):
    S, n = mesh.shape["slab"], mesh.shape["chan"]
    return jax.shard_map(
        functools.partial(body, S, n),
        mesh=mesh,
        in_specs=(P("chan", "slab", None), P(None, "chan", "slab"), P("chan", "slab", None)),
        out_specs=(P("chan", "slab", None), P("chan", "slab", None)),
        check_vma=False,
    )
```
